32 devices in a mesh: ka: 8 (over z, x), band: 4 (over y, core).
Axes of the slice: x: 2, y: 2, z: 4, core: 2. Of those that a mesh axis runs over, the one named last changes fastest.
Arguments:
- occupied: bfloat16 [16, 8, 4096], P('ka'), may hold values from -6 to 6
- virtual: bfloat16 [16, 128, 4096], P('ka', 'band'), may hold values from -6 to 6
- occ_energy: float32 [16, 8], P('ka'), may hold values from -2 to -0.5
- virt_energy: float32 [16, 128], P(None, 'band'), may hold values from 0.5 to 2
- partner: int32 [2, 16], replicated, may hold values from 0 to 15, as said below
- coulomb: float32 [2, 512], replicated, may hold values from 0.5 to 2
- basis: bfloat16 [512, 4096], replicated, may hold values from -0.09375 to 0.09375
Outputs:
- occ_update: bfloat16 [16, 8, 4096], P('ka', None, 'band')
- virt_update: bfloat16 [16, 128, 4096], P('ka', 'band')
The draws below stay inside these ranges and needn't reach their ends.
Inputs may be any that keep to these rules, and one draw needn't show every extreme that they name: Each row pairs the 16 k-points: partner[q, partner[q, k]] == k and partner[q, k] != k.
All inputs are finite; a program needn't handle non-finite values.
Results may differ from the reference program's by a relative error of at most 0.012.
Values may be sent and summed in bfloat16 or wider, within the bound.
No kernel may reach another device: no remote copies, remote signals or barrier semaphores. Data moves between devices by JAX's collectives and lax.ppermute only.
A program may use at most 64 MiB of HBM per device.

```python
import math
import jax
import jax.numpy as jnp
from jax import lax

OCC = 8
G = 4096
NAUX = 512
NQ = 2
NK = 16
VIRT = 128


def draw_partner(key, part):
    tables = []
    for transfer in range(NQ):
        order = jax.random.permutation(jax.random.fold_in(key, 101 + transfer), NK).astype(jnp.int32)
        firsts = order[0::2]
        seconds = order[1::2]
        table = jnp.zeros((NK,), jnp.int32).at[firsts].set(seconds).at[seconds].set(firsts)
        tables.append(table)
    return jnp.stack(tables).astype(jnp.int32)


def levels(stream_key, dims, split, smallest, top_value):
    factor_of, own = 1.0, jax.random.fold_in(stream_key, 6)
    for position, blocks in split:
        steps = jnp.exp(jax.random.uniform(jax.random.fold_in(own, position), (blocks,), jnp.float32, smallest / len(split), top_value / len(split)))
        factor_of = factor_of * jnp.repeat(steps, dims[position] // blocks).reshape([-1 if axis == position else 1 for axis in range(len(dims))])
    return factor_of


def scatter_about(rng, extent, spread, bound, split=(), held_as=jnp.bfloat16):
    result = jax.random.normal(rng, extent, jnp.float32) * spread
    if len(split) > 0:
        result = levels(rng, extent, split, -0.22, 0.18) * result
    return jnp.clip(result, min=-bound, max=bound).astype(held_as)


def setup_inputs(seed: int = 0) -> dict:
    keys = jax.random.split(jax.random.key(seed), 8)
    occupied = scatter_about(keys[0], (NK, OCC, G), 1.0, 6.0, ((0, 8),))
    virtual = scatter_about(keys[1], (NK, VIRT, G), 1.0, 6.0, ((0, 8), (1, 4)))
    occ_energy = jnp.clip(-2.0 + 1.5 * jax.random.uniform(keys[2], (NK, OCC), jnp.float32) ** levels(keys[2], (NK, OCC), ((0, 8),), -0.2, 0.2), -2.0, -0.5)
    virt_energy = jnp.clip(0.5 + 1.5 * jax.random.uniform(keys[3], (NK, VIRT), jnp.float32) ** levels(keys[3], (NK, VIRT), ((1, 4),), -0.2, 0.2), 0.5, 2.0)
    partner = draw_partner(jax.random.fold_in(keys[7], 71), 0)
    coulomb = jnp.clip(jnp.exp(jax.random.uniform(keys[5], (NQ, NAUX), jnp.float32, math.log(0.5), math.log(2.0))), 0.5, 2.0)
    basis = scatter_about(keys[6], (NAUX, G), G ** -0.5, 0.09375)
    return {"occupied": occupied, "virtual": virtual, "occ_energy": occ_energy, "virt_energy": virt_energy, "partner": partner, "coulomb": coulomb, "basis": basis}


FREQUENCY = 2.5
BROADENING = 0.4

def response(energy_gaps):
    shifted = FREQUENCY - energy_gaps
    return shifted / (shifted * shifted + BROADENING * BROADENING)

def contract_grid(left, right):
    return lax.dot_general(left, right, (((1,), (1,)), ((), ())), preferred_element_type=jnp.float32)

def contract_rows(left, right):
    return lax.dot_general(left, right, (((0,), (0,)), ((), ())), preferred_element_type=jnp.float32)

def reference(occupied, virtual, occ_energy, virt_energy, partner, coulomb, basis):
    gram_scale = 1.0 / math.sqrt(NK * OCC * VIRT * NAUX)
    occ_scale = 1.0 / math.sqrt(NQ * VIRT)
    occ_total = jnp.zeros((NK, OCC, G), jnp.float32)
    virt_total = jnp.zeros((NK, VIRT, G), jnp.float32)
    for transfer in range(NQ):
        partners = partner[transfer].astype(jnp.int32)
        partner_virt = jnp.take(virtual, partners, axis=0)
        partner_energy = jnp.take(virt_energy, partners, axis=0)
        weights = response(partner_energy[:, None, :] - occ_energy[:, :, None])

        def project(inputs):
            occ_k, virt_k = inputs
            pair_rows = (occ_k[:, None, :] * virt_k[None, :, :]).reshape(OCC * VIRT, G)
            return contract_grid(pair_rows, basis).astype(jnp.bfloat16)
        coeffs = lax.map(project, (occupied, partner_virt))
        flat_coeffs = coeffs.reshape(NK * OCC * VIRT, NAUX)
        weighted = (flat_coeffs.astype(jnp.float32) * weights.reshape(-1, 1)).astype(jnp.bfloat16)
        gram_block = contract_rows(weighted, flat_coeffs)
        screen_block = (coulomb[transfer][:, None] * gram_block * coulomb[transfer][None, :] * gram_scale).astype(jnp.bfloat16)

        def respond(inputs):
            coeff_k, occ_k, virt_k = inputs
            screened = jnp.dot(coeff_k, screen_block, preferred_element_type=jnp.float32).astype(jnp.bfloat16)
            grid_field = jnp.dot(screened, basis, preferred_element_type=jnp.float32).astype(jnp.bfloat16)
            grid_field = grid_field.reshape(OCC, VIRT, G).astype(jnp.float32)
            occ_term = lax.optimization_barrier(jnp.sum(grid_field * virt_k.astype(jnp.float32)[None, :, :], axis=1))
            virt_term = lax.optimization_barrier(jnp.sum(grid_field * occ_k.astype(jnp.float32)[:, None, :], axis=0)).astype(jnp.bfloat16)
            return (occ_term, virt_term)
        occ_term, virt_term = lax.map(respond, (coeffs, occupied, partner_virt))
        occ_total = occ_total + occ_term
        virt_total = virt_total + jnp.take(virt_term, partners, axis=0).astype(jnp.float32)
    return ((occ_total * occ_scale).astype(jnp.bfloat16), virt_total.astype(jnp.bfloat16))
```

```python
import math

import jax
import jax.numpy as jnp
from jax import lax
from jax.sharding import PartitionSpec as P

FREQUENCY = 2.5
BROADENING = 0.4
LANES = 128
BF16 = jnp.bfloat16
F32 = jnp.float32


def response(energy_gaps):
    shifted = FREQUENCY - energy_gaps
    return shifted / (shifted * shifted + BROADENING * BROADENING)


def pick(stack, index):
    return lax.dynamic_index_in_dim(stack, index, 0, keepdims=False)


class Hypercube:
    def __init__(self):
        self.ka = lax.axis_size("ka")
        self.band = lax.axis_size("band")
        self.count = self.ka * self.band
        assert self.band == 4 and self.ka >= 2 and self.ka & (self.ka - 1) == 0
        self.index = lax.axis_index("ka") * self.band + lax.axis_index("band")
        self.core, self.y, self.x = 1, 2, 4
        rest = [bit for bit in (1 << n for n in range(3, 31)) if bit < self.count]
        self.groups = [rest[n : n + 2] for n in range(0, len(rest), 2)]

    def bit(self, mask):
        return (self.index // mask) % 2

    def swap(self, value, mask):
        return lax.ppermute(
            value, ("ka", "band"), [(device, device ^ mask) for device in range(self.count)]
        )


def masks_of(bits):
    return [sum(bit for n, bit in enumerate(bits) if (d >> n) & 1) for d in range(1, 1 << len(bits))]


def sum_scatter(cube, parts, bits):
    me = sum(cube.bit(bit) << n for n, bit in enumerate(bits))
    total = pick(parts, me).astype(F32)
    arrived = [
        cube.swap(pick(parts, jnp.bitwise_xor(me, d + 1)), mask)
        for d, mask in enumerate(masks_of(bits))
    ]
    for term in arrived:
        total = total + term.astype(F32)
    return total


def gather_differences(cube, value, bits):
    return jnp.stack([value] + [cube.swap(value, mask) for mask in masks_of(bits)])


def gather_parts(cube, value, bits):
    me = sum(cube.bit(bit) << n for n, bit in enumerate(bits))
    differences = gather_differences(cube, value, bits)
    return jnp.stack(
        [pick(differences, jnp.bitwise_xor(me, d)) for d in range(1 << len(bits))]
    )


def blocks_of(aux_count):
    count = aux_count // LANES
    return [(row, column) for row in range(count) for column in range(row, count)]


def pack_upper(gram):
    return jnp.stack(
        [
            gram[row * LANES : (row + 1) * LANES, column * LANES : (column + 1) * LANES]
            for row, column in blocks_of(gram.shape[0])
        ]
    )


def unpack_upper(packed, aux_count):
    count = aux_count // LANES
    where = {pair: n for n, pair in enumerate(blocks_of(aux_count))}
    return jnp.concatenate(
        [
            jnp.concatenate(
                [
                    packed[where[row, column]]
                    if row <= column
                    else packed[where[column, row]].T
                    for column in range(count)
                ],
                axis=1,
            )
            for row in range(count)
        ],
        axis=0,
    )


def split_float(value):
    high = lax.reduce_precision(value, 8, 7)
    middle = lax.reduce_precision(value - high, 8, 7)
    low = value - high - middle
    return high.astype(BF16), middle.astype(BF16), low.astype(BF16)


def fetch_partners(cube, occupied, occ_energy, partner):
    local_k, occ_count, grid_count = occupied.shape
    transfers = partner.shape[0]
    width = grid_count // cube.band
    ka = lax.axis_index("ka")
    quarter = lax.dynamic_slice_in_dim(occupied, lax.axis_index("band") * width, width, axis=2)
    pieces = jnp.stack(split_float(occ_energy), axis=2)
    payload = jnp.concatenate(
        [quarter, jnp.pad(pieces, ((0, 0), (0, 0), (0, LANES - pieces.shape[2])))], axis=2
    )
    gathered = payload[None]
    for bits in cube.groups:
        gathered = gather_differences(cube, gathered, bits).reshape((-1,) + payload.shape)
    gathered = gathered.reshape((-1,) + payload.shape[1:])
    side, upper = ka % 2, ka // 2

    def wanted(target_side):
        target = (upper * 2 + target_side) * local_k
        sources = lax.dynamic_slice_in_dim(partner, target, local_k, axis=1)
        devices = sources // local_k
        slots = jnp.bitwise_xor(devices // 2, upper) * local_k + sources % local_k
        rows = [
            pick(gathered, slots[transfer, k])
            for transfer in range(transfers)
            for k in range(local_k)
        ]
        return jnp.stack(rows), devices % 2

    mine, sides = wanted(side)
    theirs, _ = wanted(1 - side)
    received = cube.swap(theirs, cube.x)
    chosen = jnp.where((sides == side).reshape(-1, 1, 1), mine, received)
    energy = chosen[:, :, width : width + 3].astype(F32)
    energy = (energy[:, :, 0] + energy[:, :, 1]) + energy[:, :, 2]
    part = chosen[:, :, :width]
    for mask in (cube.core, cube.y):
        other = cube.swap(part, mask)
        first = cube.bit(mask) == 0
        part = jnp.concatenate(
            [jnp.where(first, part, other), jnp.where(first, other, part)], axis=2
        )
    shape = (transfers, local_k, occ_count)
    return part.reshape(shape + (grid_count,)), energy.reshape(shape)


def reduce_screen(cube, packed, coulomb, scale):
    transfers, aux_count = coulomb.shape
    core = cube.bit(cube.core)
    own = sum_scatter(cube, packed, [cube.core]).astype(BF16)
    rows = own.shape[0] * LANES
    piece = sum_scatter(cube, own.reshape(4, rows // 4, LANES), [cube.y, cube.x])
    for bits in cube.groups:
        piece = piece.astype(BF16)
        arrived = [cube.swap(piece, mask) for mask in masks_of(bits)]
        piece = piece.astype(F32)
        for term in arrived:
            piece = piece + term.astype(F32)
    factors = pick(coulomb, core)
    scales = pack_upper(factors[:, None] * factors[None, :] * scale).reshape(4, rows // 4, LANES)
    me = cube.bit(cube.y) + 2 * cube.bit(cube.x)
    piece = (piece * pick(scales, me)).astype(BF16)
    own = gather_parts(cube, piece, [cube.y, cube.x])
    both = gather_parts(cube, own, [cube.core])
    return both.reshape(packed.shape)


def return_occupied(cube, terms, partner):
    transfers, local_k, occ_count, grid_count = terms.shape
    ka = lax.axis_index("ka")
    part = terms.reshape(transfers * local_k, occ_count, grid_count).astype(BF16)
    for mask in (cube.y, cube.core):
        width = part.shape[2] // 2
        bit = cube.bit(mask)
        keep = lax.dynamic_slice_in_dim(part, bit * width, width, axis=2)
        give = lax.dynamic_slice_in_dim(part, (1 - bit) * width, width, axis=2)
        part = (keep.astype(F32) + cube.swap(give, mask).astype(F32)).astype(BF16)
    side, upper = ka % 2, ka // 2
    received = cube.swap(part, cube.x)
    both = jnp.stack([part, received]).reshape((2 * transfers * local_k,) + part.shape[1:])
    devices = jnp.stack([ka, jnp.bitwise_xor(ka, 1)])
    own_k = devices[:, None] * local_k + jnp.arange(local_k, dtype=jnp.int32)[None]
    targets = jnp.take(partner, own_k, axis=1).transpose(1, 0, 2).reshape(-1)

    def placed(uppers):
        wanted_k = ((uppers * 2 + side) * local_k)[:, None] + jnp.arange(local_k, dtype=jnp.int32)
        hits = targets[None, None, :] == wanted_k[:, :, None]
        return jnp.sum(
            jnp.where(hits[:, :, :, None, None], both[None, None].astype(F32), 0.0), axis=2
        )

    spans = 1
    for bits in cube.groups:
        spans *= 1 << len(bits)
    differences = jnp.arange(spans, dtype=jnp.int32)
    value = placed(jnp.bitwise_xor(differences, upper))
    for bits in reversed(cube.groups):
        size = 1 << len(bits)
        value = value.reshape((size, -1) + value.shape[1:])
        total = value[0]
        arrived = [
            cube.swap(value[d + 1].astype(BF16), mask) for d, mask in enumerate(masks_of(bits))
        ]
        for term in arrived:
            total = total + term.astype(F32)
        value = total
    return value[0]


def contract_grid(left, right):
    return lax.dot_general(left, right, (((1,), (1,)), ((), ())), preferred_element_type=F32)


def contract_rows(left, right):
    return lax.dot_general(left, right, (((0,), (0,)), ((), ())), preferred_element_type=F32)


def shards(occupied, virtual, occ_energy, virt_energy, partner, coulomb, basis):
    local_k, occ_count, grid_count = occupied.shape
    group_count = virtual.shape[1]
    aux_count = basis.shape[0]
    transfers = partner.shape[0]
    cube = Hypercube()
    total_k = local_k * cube.ka
    virt_count = group_count * cube.band
    gram_scale = 1.0 / math.sqrt(total_k * occ_count * virt_count * aux_count)
    occ_scale = 1.0 / math.sqrt(transfers * virt_count)
    ka = lax.axis_index("ka")

    partner_occ, partner_energy = fetch_partners(cube, occupied, occ_energy, partner)
    own_energy = lax.dynamic_slice_in_dim(virt_energy, ka * local_k, local_k, axis=0)
    coeffs, grams = [], []
    for transfer in range(transfers):
        pair_rows = partner_occ[transfer][:, :, None, :] * virtual[:, None, :, :]
        pair_coeffs = contract_grid(pair_rows.reshape(-1, grid_count), basis).astype(BF16)
        gaps = own_energy[:, None, :] - partner_energy[transfer][:, :, None]
        weights = response(gaps).reshape(-1, 1)
        weighted = (pair_coeffs.astype(F32) * weights).astype(BF16)
        grams.append(pack_upper(contract_rows(weighted, pair_coeffs)).astype(BF16))
        coeffs.append(pair_coeffs)
    screens = reduce_screen(cube, jnp.stack(grams), coulomb, gram_scale)
    virt_total = jnp.zeros((local_k, group_count, grid_count), F32)
    occ_terms = []
    for transfer in range(transfers):
        screen = unpack_upper(screens[transfer], aux_count)
        screened = jnp.dot(coeffs[transfer], screen, preferred_element_type=F32).astype(BF16)
        field = jnp.dot(screened, basis, preferred_element_type=F32).astype(BF16)
        field = field.reshape(local_k, occ_count, group_count, grid_count).astype(F32)
        occ_terms.append(jnp.sum(field * virtual[:, None].astype(F32), axis=2))
        virt_term = jnp.sum(field * partner_occ[transfer][:, :, None, :].astype(F32), axis=1)
        virt_total = virt_total + virt_term.astype(BF16).astype(F32)
    occ_total = return_occupied(cube, jnp.stack(occ_terms), partner)
    return ((occ_total * occ_scale).astype(BF16), virt_total.astype(BF16))


def solution(mesh):
    in_specs = (
        P("ka", None, None),
        P("ka", "band", None),
        P("ka", None),
        P(None, "band"),
        P(),
        P(),
        P(),
    )
    out_specs = (P("ka", None, "band"), P("ka", "band", None))
    return jax.shard_map(shards, mesh=mesh, in_specs=in_specs, out_specs=out_specs, check_vma=False)
```

```python
import functools
import math

import jax
import jax.numpy as jnp
from jax import lax
from jax.experimental import pallas as pl
from jax.experimental.pallas import tpu as pltpu
from jax.sharding import PartitionSpec as P

FREQUENCY = 2.5
BROADENING = 0.4
LANES = 128
BF16 = jnp.bfloat16
F32 = jnp.float32


def response(energy_gaps):
    shifted = FREQUENCY - energy_gaps
    return shifted / (shifted * shifted + BROADENING * BROADENING)


def pick(stack, index):
    return lax.dynamic_index_in_dim(stack, index, 0, keepdims=False)


class Hypercube:
    def __init__(self):
        self.ka = lax.axis_size("ka")
        self.band = lax.axis_size("band")
        self.count = self.ka * self.band
        assert self.band == 4 and self.ka >= 2 and self.ka & (self.ka - 1) == 0
        self.index = lax.axis_index("ka") * self.band + lax.axis_index("band")
        self.core, self.y, self.x = 1, 2, 4
        rest = [bit for bit in (1 << n for n in range(3, 31)) if bit < self.count]
        self.groups = [rest[n : n + 2] for n in range(0, len(rest), 2)]

    def bit(self, mask):
        return (self.index // mask) % 2

    def swap(self, value, mask):
        return lax.ppermute(
            value, ("ka", "band"), [(device, device ^ mask) for device in range(self.count)]
        )


def masks_of(bits):
    return [sum(bit for n, bit in enumerate(bits) if (d >> n) & 1) for d in range(1, 1 << len(bits))]


def sum_scatter(cube, parts, bits):
    me = sum(cube.bit(bit) << n for n, bit in enumerate(bits))
    total = pick(parts, me).astype(F32)
    arrived = [
        cube.swap(pick(parts, jnp.bitwise_xor(me, d + 1)), mask)
        for d, mask in enumerate(masks_of(bits))
    ]
    for term in arrived:
        total = total + term.astype(F32)
    return total


def gather_differences(cube, value, bits):
    return jnp.stack([value] + [cube.swap(value, mask) for mask in masks_of(bits)])


def gather_parts(cube, value, bits):
    me = sum(cube.bit(bit) << n for n, bit in enumerate(bits))
    differences = gather_differences(cube, value, bits)
    return jnp.stack(
        [pick(differences, jnp.bitwise_xor(me, d)) for d in range(1 << len(bits))]
    )


def blocks_of(aux_count):
    count = aux_count // LANES
    return [(row, column) for row in range(count) for column in range(row, count)]


def split_float(value):
    high = lax.reduce_precision(value, 8, 7)
    middle = lax.reduce_precision(value - high, 8, 7)
    low = value - high - middle
    return high.astype(BF16), middle.astype(BF16), low.astype(BF16)


def fetch_partners(cube, occupied, occ_energy, partner):
    local_k, occ_count, grid_count = occupied.shape
    width = grid_count // cube.band
    ka = lax.axis_index("ka")
    quarter = lax.dynamic_slice_in_dim(occupied, lax.axis_index("band") * width, width, axis=2)
    pieces = jnp.stack(split_float(occ_energy), axis=2)
    payload = jnp.concatenate(
        [quarter, jnp.pad(pieces, ((0, 0), (0, 0), (0, LANES - pieces.shape[2])))], axis=2
    )
    gathered = payload[None]
    for bits in cube.groups:
        gathered = gather_differences(cube, gathered, bits).reshape((-1,) + payload.shape)
    gathered = gathered.reshape((-1,) + payload.shape[1:])
    side, upper = ka % 2, ka // 2
    slots = jnp.arange(gathered.shape[0], dtype=jnp.int32)
    held = (jnp.bitwise_xor(slots // local_k, upper) * 2 + side) * local_k + slots % local_k
    every_k = jnp.arange(partner.shape[1], dtype=jnp.int32)

    def wanted(target_side):
        targets = (upper * 2 + target_side) * local_k + jnp.arange(local_k, dtype=jnp.int32)
        at_target = every_k[None, None, :] == targets[None, :, None]
        sources = jnp.sum(jnp.where(at_target, partner[:, None, :], 0), axis=2).reshape(-1)
        hits = sources[:, None] == held[None, :]
        rows = jnp.sum(
            jnp.where(hits[:, :, None, None], gathered[None].astype(F32), 0.0), axis=1
        ).astype(BF16)
        return rows

    mine = wanted(side)
    theirs = wanted(1 - side)
    received = cube.swap(theirs, cube.x)
    chosen = mine + received
    energy = chosen[:, :, width : width + 3].astype(F32)
    energy = (energy[:, :, 0] + energy[:, :, 1]) + energy[:, :, 2]
    part = chosen[:, :, :width]
    for mask in (cube.core, cube.y):
        other = cube.swap(part, mask)
        first = cube.bit(mask) == 0
        part = jnp.concatenate(
            [jnp.where(first, part, other), jnp.where(first, other, part)], axis=2
        )
    return part, energy


def reduce_screen(cube, packed):
    own = sum_scatter(cube, packed, [cube.core]).astype(BF16)
    rows = own.shape[0] * LANES
    piece = sum_scatter(cube, own.reshape(4, rows // 4, LANES), [cube.y, cube.x]).astype(BF16)
    for bits in cube.groups:
        arrived = [cube.swap(piece, mask) for mask in masks_of(bits)]
        total = piece.astype(F32)
        for term in arrived:
            total = total + term.astype(F32)
        piece = total.astype(BF16)
    own = gather_parts(cube, piece, [cube.y, cube.x])
    return gather_parts(cube, own, [cube.core]).reshape(packed.shape)


def return_occupied(cube, terms, partner):
    transfers, local_k, occ_count, grid_count = terms.shape
    ka = lax.axis_index("ka")
    part = terms.reshape(transfers * local_k, occ_count, grid_count).astype(BF16)
    for mask in (cube.y, cube.core):
        width = part.shape[2] // 2
        bit = cube.bit(mask)
        keep = lax.dynamic_slice_in_dim(part, bit * width, width, axis=2)
        give = lax.dynamic_slice_in_dim(part, (1 - bit) * width, width, axis=2)
        part = (keep.astype(F32) + cube.swap(give, mask).astype(F32)).astype(BF16)
    side, upper = ka % 2, ka // 2
    received = cube.swap(part, cube.x)
    both = jnp.stack([part, received]).reshape((2 * transfers * local_k,) + part.shape[1:])
    devices = jnp.stack([ka, jnp.bitwise_xor(ka, 1)])
    own_k = devices[:, None] * local_k + jnp.arange(local_k, dtype=jnp.int32)[None]
    targets = jnp.take(partner, own_k, axis=1).transpose(1, 0, 2).reshape(-1)

    def placed(uppers):
        wanted_k = ((uppers * 2 + side) * local_k)[:, None] + jnp.arange(local_k, dtype=jnp.int32)
        hits = targets[None, None, :] == wanted_k[:, :, None]
        return jnp.sum(
            jnp.where(hits[:, :, :, None, None], both[None, None].astype(F32), 0.0), axis=2
        )

    spans = 1
    for bits in cube.groups:
        spans *= 1 << len(bits)
    differences = jnp.arange(spans, dtype=jnp.int32)
    value = placed(jnp.bitwise_xor(differences, upper))
    for bits in reversed(cube.groups):
        size = 1 << len(bits)
        value = value.reshape((size, -1) + value.shape[1:])
        total = value[0]
        arrived = [
            cube.swap(value[d + 1].astype(BF16), mask) for d, mask in enumerate(masks_of(bits))
        ]
        for term in arrived:
            total = total + term.astype(F32)
        value = total
    return value[0]


def project_kernel(
    occ_ref, virt_ref, basis_ref, occ_energy_ref, virt_energy_ref, coulomb_ref,
    coeffs_ref, gram_ref, weighted_ref, *, scale,
):
    terms, occ_count, _ = occ_ref.shape
    local_k, group_count, _ = virt_ref.shape
    aux_count = basis_ref.shape[0]
    rows = occ_count * group_count
    per_transfer = local_k * rows
    count = aux_count // LANES
    for transfer in range(terms // local_k):
        for k in range(local_k):
            term = transfer * local_k + k
            virt = virt_ref[k]
            occ = occ_ref[term]
            pair_rows = jnp.concatenate([occ[i : i + 1] * virt for i in range(occ_count)], axis=0)
            coeffs = lax.dot_general(
                pair_rows, basis_ref[...], (((1,), (1,)), ((), ())), preferred_element_type=F32
            ).astype(BF16)
            coeffs_ref[term * rows : (term + 1) * rows, :] = coeffs
            for i in range(occ_count):
                start = i * group_count
                weights = response(virt_energy_ref[k] - occ_energy_ref[term][i : i + 1])
                values = coeffs[start : start + group_count].astype(F32)
                weighted_ref[k * rows + start : k * rows + start + group_count, :] = (
                    jnp.concatenate(
                        [values[:, n * LANES : (n + 1) * LANES] * weights for n in range(count)],
                        axis=1,
                    ).astype(BF16)
                )
        where = slice(transfer * per_transfer, (transfer + 1) * per_transfer)
        coulomb = coulomb_ref[transfer : transfer + 1, :] * math.sqrt(scale)
        for panel in range(0, count, 2):
            height = min(2, count - panel)
            gram = lax.dot_general(
                weighted_ref[:, panel * LANES : (panel + height) * LANES],
                coeffs_ref[where, panel * LANES :],
                (((0,), (0,)), ((), ())),
                preferred_element_type=F32,
            )
            for n, (row, column) in enumerate(blocks_of(aux_count)):
                if not panel <= row < panel + height:
                    continue
                down, across = (row - panel) * LANES, (column - panel) * LANES
                tile = gram[down : down + LANES, across : across + LANES]
                first = jnp.broadcast_to(
                    coulomb[:, row * LANES : (row + 1) * LANES], (LANES, LANES)
                ).T
                second = coulomb[:, column * LANES : (column + 1) * LANES]
                gram_ref[transfer, n] = (first * tile * second).astype(BF16)


def project(occ, virtual, basis, occ_energy, virt_energy, coulomb, scale):
    terms, occ_count, grid_count = occ.shape
    local_k, group_count, _ = virtual.shape
    aux_count = basis.shape[0]
    transfers = terms // local_k
    rows = terms * occ_count * group_count
    blocks = len(blocks_of(aux_count))
    return pl.pallas_call(
        functools.partial(project_kernel, scale=scale),
        in_specs=[pl.BlockSpec(memory_space=pltpu.VMEM)] * 6,
        out_specs=[pl.BlockSpec(memory_space=pltpu.VMEM)] * 2,
        out_shape=[
            jax.ShapeDtypeStruct((rows, aux_count), BF16),
            jax.ShapeDtypeStruct((transfers, blocks, LANES, LANES), BF16),
        ],
        scratch_shapes=[pltpu.VMEM((rows // transfers, aux_count), BF16)],
        compiler_params=pltpu.CompilerParams(vmem_limit_bytes=24 << 20),
        cost_estimate=pl.CostEstimate(
            flops=2 * rows * grid_count * aux_count, bytes_accessed=8 << 20, transcendentals=0
        ),
        name="project",
    )(occ, virtual, basis, occ_energy, virt_energy, coulomb)


def respond_kernel(
    coeffs_ref, packed_ref, basis_ref, occ_ref, virt_ref,
    term_ref, update_ref, screen_ref, screened_ref,
):
    terms, occ_count, _ = occ_ref.shape
    local_k, group_count, _ = virt_ref.shape
    aux_count = basis_ref.shape[0]
    rows = occ_count * group_count
    transfers = terms // local_k

    @pl.when(pl.program_id(0) == 0)
    def _():
        for transfer in range(transfers):
            for n, (row, column) in enumerate(blocks_of(aux_count)):
                tile = packed_ref[transfer, n]
                upper = slice(row * LANES, (row + 1) * LANES)
                lower = slice(column * LANES, (column + 1) * LANES)
                screen_ref[upper, lower] = tile
                if row != column:
                    screen_ref[lower, upper] = tile.T
            where = slice(transfer * local_k * rows, (transfer + 1) * local_k * rows)
            screened_ref[where, :] = jnp.dot(
                coeffs_ref[where, :], screen_ref[...], preferred_element_type=F32
            ).astype(BF16)

    for k in range(local_k):
        virt = virt_ref[k].astype(F32)
        total = None
        for transfer in range(transfers):
            term = transfer * local_k + k
            field = jnp.dot(
                screened_ref[term * rows : (term + 1) * rows, :],
                basis_ref[...],
                preferred_element_type=F32,
            ).astype(BF16)
            occ = occ_ref[term].astype(F32)
            virt_term = None
            lines = []
            for i in range(occ_count):
                piece = field[i * group_count : (i + 1) * group_count].astype(F32)
                lines.append(jnp.sum(piece * virt, axis=0, keepdims=True))
                product = piece * occ[i : i + 1]
                virt_term = product if virt_term is None else virt_term + product
            term_ref[term] = jnp.concatenate(lines, axis=0).astype(BF16)
            virt_term = virt_term.astype(BF16).astype(F32)
            total = virt_term if total is None else total + virt_term
        update_ref[k] = total.astype(BF16)


def respond(coeffs, packed, basis, occ, virtual):
    terms, occ_count, grid_count = occ.shape
    local_k, group_count, _ = virtual.shape
    aux_count = basis.shape[0]
    rows = coeffs.shape[0]
    width = min(1024, grid_count)
    return pl.pallas_call(
        respond_kernel,
        grid=(grid_count // width,),
        in_specs=[
            pl.BlockSpec(coeffs.shape, lambda n: (0, 0)),
            pl.BlockSpec(packed.shape, lambda n: (0, 0, 0, 0)),
            pl.BlockSpec((aux_count, width), lambda n: (0, n)),
            pl.BlockSpec((terms, occ_count, width), lambda n: (0, 0, n)),
            pl.BlockSpec((local_k, group_count, width), lambda n: (0, 0, n)),
        ],
        out_specs=[
            pl.BlockSpec((terms, occ_count, width), lambda n: (0, 0, n)),
            pl.BlockSpec((local_k, group_count, width), lambda n: (0, 0, n)),
        ],
        out_shape=[
            jax.ShapeDtypeStruct(occ.shape, BF16),
            jax.ShapeDtypeStruct(virtual.shape, BF16),
        ],
        scratch_shapes=[
            pltpu.VMEM((aux_count, aux_count), BF16),
            pltpu.VMEM((rows, aux_count), BF16),
        ],
        compiler_params=pltpu.CompilerParams(vmem_limit_bytes=24 << 20),
        cost_estimate=pl.CostEstimate(
            flops=2 * rows * grid_count * aux_count, bytes_accessed=8 << 20, transcendentals=0
        ),
        name="respond",
    )(coeffs, packed, basis, occ, virtual)


def shards(occupied, virtual, occ_energy, virt_energy, partner, coulomb, basis):
    local_k, occ_count, grid_count = occupied.shape
    group_count = virtual.shape[1]
    aux_count = basis.shape[0]
    transfers = partner.shape[0]
    cube = Hypercube()
    total_k = local_k * cube.ka
    virt_count = group_count * cube.band
    gram_scale = 1.0 / math.sqrt(total_k * occ_count * virt_count * aux_count)
    occ_scale = 1.0 / math.sqrt(transfers * virt_count)
    ka = lax.axis_index("ka")

    own_energy = lax.dynamic_slice_in_dim(virt_energy, ka * local_k, local_k, axis=0)
    own_energy = jnp.broadcast_to(own_energy[:, :, None], own_energy.shape + (LANES,))
    partner_occ, partner_energy = fetch_partners(cube, occupied, occ_energy, partner)
    partner_energy = jnp.broadcast_to(
        partner_energy[:, :, None], partner_energy.shape + (LANES,)
    )
    coeffs, packed = project(
        partner_occ, virtual, basis, partner_energy, own_energy, coulomb, gram_scale
    )
    packed = reduce_screen(cube, packed)
    terms, virt_update = respond(coeffs, packed, basis, partner_occ, virtual)
    terms = terms.reshape(transfers, local_k, occ_count, grid_count)
    occ_total = return_occupied(cube, terms, partner)
    return ((occ_total * occ_scale).astype(BF16), virt_update)


def solution(mesh):
    in_specs = (
        P("ka", None, None),
        P("ka", "band", None),
        P("ka", None),
        P(None, "band"),
        P(),
        P(),
        P(),
    )
    out_specs = (P("ka", None, "band"), P("ka", "band", None))
    return jax.shard_map(shards, mesh=mesh, in_specs=in_specs, out_specs=out_specs, check_vma=False)
```

```python
import functools
import math

import jax
import jax.numpy as jnp
from jax import lax
from jax.experimental import pallas as pl
from jax.experimental.pallas import tpu as pltpu
from jax.sharding import PartitionSpec as P

FREQUENCY = 2.5
BROADENING = 0.4
LANES = 128
KERNEL_VMEM = 50 << 20
VMEM_SPEC = pl.BlockSpec(memory_space=pltpu.VMEM)
BF16 = jnp.bfloat16
F32 = jnp.float32


def response(energy_gaps):
    shifted = FREQUENCY - energy_gaps
    return shifted / (shifted * shifted + BROADENING * BROADENING)


def pick(stack, index):
    return lax.dynamic_index_in_dim(stack, index, 0, keepdims=False)


class Hypercube:
    def __init__(self):
        self.ka = lax.axis_size("ka")
        self.band = lax.axis_size("band")
        self.count = self.ka * self.band
        assert self.band == 4 and self.ka >= 2 and self.ka & (self.ka - 1) == 0
        self.index = lax.axis_index("ka") * self.band + lax.axis_index("band")
        self.core, self.y, self.x = 1, 2, 4
        rest = [bit for bit in (1 << n for n in range(3, 31)) if bit < self.count]
        self.groups = [rest[n : n + 2] for n in range(0, len(rest), 2)]

    def bit(self, mask):
        return (self.index // mask) % 2

    def swap(self, value, mask):
        return lax.ppermute(
            value, ("ka", "band"), [(device, device ^ mask) for device in range(self.count)]
        )


def masks_of(bits):
    return [sum(bit for n, bit in enumerate(bits) if (d >> n) & 1) for d in range(1, 1 << len(bits))]


def sum_scatter(cube, parts, bits):
    me = sum(cube.bit(bit) << n for n, bit in enumerate(bits))
    total = pick(parts, me).astype(F32)
    arrived = [
        cube.swap(pick(parts, jnp.bitwise_xor(me, d + 1)), mask)
        for d, mask in enumerate(masks_of(bits))
    ]
    for term in arrived:
        total = total + term.astype(F32)
    return total


def gather_differences(cube, value, bits):
    return jnp.stack([value] + [cube.swap(value, mask) for mask in masks_of(bits)])


def gather_parts(cube, value, bits):
    me = sum(cube.bit(bit) << n for n, bit in enumerate(bits))
    differences = gather_differences(cube, value, bits)
    return jnp.stack(
        [pick(differences, jnp.bitwise_xor(me, d)) for d in range(1 << len(bits))]
    )


def blocks_of(aux_count):
    count = aux_count // LANES
    return [(row, column) for row in range(count) for column in range(row, count)]


def split_float(value):
    high = lax.reduce_precision(value, 8, 7)
    middle = lax.reduce_precision(value - high, 8, 7)
    low = value - high - middle
    return high.astype(BF16), middle.astype(BF16), low.astype(BF16)


def partners_of(partner, device, local_k):
    every_k = jnp.arange(partner.shape[1], dtype=jnp.int32)
    own_k = device * local_k + jnp.arange(local_k, dtype=jnp.int32)
    here = every_k[None, None, :] == own_k[None, :, None]
    return jnp.sum(jnp.where(here, partner[:, None, :], 0), axis=2).reshape(-1)


def fetch_partners(cube, occupied, occ_energy, sources, neighbour_sources):
    local_k, occ_count, grid_count = occupied.shape
    width = grid_count // 2
    ka = lax.axis_index("ka")
    first = cube.bit(cube.core) == 0
    half = jnp.where(first, occupied[:, :, :width], occupied[:, :, width:])
    pieces = jnp.stack(split_float(occ_energy), axis=2)
    payload = jnp.concatenate(
        [half, jnp.pad(pieces, ((0, 0), (0, 0), (0, LANES - pieces.shape[2])))], axis=2
    )
    gathered = payload[None]
    for bits in cube.groups:
        gathered = gather_differences(cube, gathered, bits).reshape((-1,) + payload.shape)
    gathered = gathered.reshape((-1,) + payload.shape[1:])
    side, upper = ka % 2, ka // 2
    slots = jnp.arange(gathered.shape[0], dtype=jnp.int32)
    held = (jnp.bitwise_xor(slots // local_k, upper) * 2 + side) * local_k + slots % local_k

    def held_of(wanted):
        hits = wanted[:, None] == held[None, :]
        return jnp.sum(
            jnp.where(hits[:, :, None, None], gathered[None].astype(F32), 0.0), axis=1
        ).astype(BF16)

    chosen = held_of(sources) + cube.swap(held_of(neighbour_sources), cube.x)
    energy = chosen[:, :, width : width + 3].astype(F32)
    energy = (energy[:, :, 0] + energy[:, :, 1]) + energy[:, :, 2]
    part = chosen[:, :, :width]
    other = cube.swap(part, cube.core)
    part = jnp.concatenate([jnp.where(first, part, other), jnp.where(first, other, part)], axis=2)
    return part, energy


def reduce_screen(cube, packed):
    own = sum_scatter(cube, packed, [cube.core]).astype(BF16)
    rows = own.shape[0] * LANES
    piece = sum_scatter(cube, own.reshape(4, rows // 4, LANES), [cube.y, cube.x]).astype(BF16)
    for bits in cube.groups:
        arrived = [cube.swap(piece, mask) for mask in masks_of(bits)]
        total = piece.astype(F32)
        for term in arrived:
            total = total + term.astype(F32)
        piece = total.astype(BF16)
    own = gather_parts(cube, piece, [cube.y, cube.x])
    return gather_parts(cube, own, [cube.core]).reshape(packed.shape)


def return_occupied(cube, part, local_k, targets, neighbour_targets):
    ka = lax.axis_index("ka")
    width = part.shape[2] // 2
    first = cube.bit(cube.core) == 0
    keep = jnp.where(first, part[:, :, :width], part[:, :, width:])
    give = jnp.where(first, part[:, :, width:], part[:, :, :width])
    part = (keep.astype(F32) + cube.swap(give, cube.core).astype(F32)).astype(BF16)
    side, upper = ka % 2, ka // 2
    received = cube.swap(part, cube.x)
    both = jnp.concatenate([part, received], axis=0)
    targets = jnp.concatenate([targets, neighbour_targets])

    def placed(uppers):
        wanted_k = ((uppers * 2 + side) * local_k)[:, None] + jnp.arange(local_k, dtype=jnp.int32)
        hits = targets[None, None, :] == wanted_k[:, :, None]
        return jnp.sum(
            jnp.where(hits[:, :, :, None, None], both[None, None].astype(F32), 0.0), axis=2
        )

    spans = 1
    for bits in cube.groups:
        spans *= 1 << len(bits)
    differences = jnp.arange(spans, dtype=jnp.int32)
    value = placed(jnp.bitwise_xor(differences, upper))
    for bits in reversed(cube.groups):
        size = 1 << len(bits)
        value = value.reshape((size, -1) + value.shape[1:])
        total = value[0]
        arrived = [
            cube.swap(value[d + 1].astype(BF16), mask) for d, mask in enumerate(masks_of(bits))
        ]
        for term in arrived:
            total = total + term.astype(F32)
        value = total
    return value[0]


def grid_copies(basis_ref, held_ref, sems, starts):
    ends = starts[1:] + [basis_ref.shape[1]]
    return [
        pltpu.make_async_copy(
            basis_ref.at[:, start:end], held_ref.at[:, start:end], sems.at[n]
        )
        for n, (start, end) in enumerate(zip(starts, ends))
    ]


def project_kernel(
    occ_ref, virt_ref, occ_energy_ref, virt_energy_ref, coulomb_ref, basis_ref,
    coeffs_ref, gram_ref, weighted_ref, held_ref, total_ref, sems, *, scale,
):
    terms, occ_count, grid_count = occ_ref.shape
    local_k, group_count, _ = virt_ref.shape
    aux_count = basis_ref.shape[0]
    rows = occ_count * group_count
    per_transfer = local_k * rows
    count = aux_count // LANES
    starts = [0, grid_count // 8]
    copies = grid_copies(basis_ref, held_ref, sems, starts)
    for copy in copies:
        copy.start()

    def contract(term, start, end):
        virt = virt_ref[term % local_k, :, start:end]
        occ = occ_ref[term, :, start:end]
        pair_rows = jnp.concatenate([occ[i : i + 1] * virt for i in range(occ_count)], axis=0)
        return lax.dot_general(
            pair_rows, held_ref[:, start:end], (((1,), (1,)), ((), ())), preferred_element_type=F32
        )

    copies[0].wait()
    for term in range(terms):
        total_ref[term * rows : (term + 1) * rows, :] = contract(term, 0, starts[1])
    copies[1].wait()
    for transfer in range(terms // local_k):
        for k in range(local_k):
            term = transfer * local_k + k
            here = slice(term * rows, (term + 1) * rows)
            coeffs = (total_ref[here, :] + contract(term, starts[1], grid_count)).astype(BF16)
            coeffs_ref[here, :] = coeffs
            for i in range(occ_count):
                start = i * group_count
                weights = response(virt_energy_ref[k] - occ_energy_ref[term][i : i + 1])
                values = coeffs[start : start + group_count].astype(F32)
                weighted_ref[k * rows + start : k * rows + start + group_count, :] = (
                    jnp.concatenate(
                        [values[:, n * LANES : (n + 1) * LANES] * weights for n in range(count)],
                        axis=1,
                    ).astype(BF16)
                )
        where = slice(transfer * per_transfer, (transfer + 1) * per_transfer)
        coulomb = coulomb_ref[transfer : transfer + 1, :] * math.sqrt(scale)
        for panel in range(0, count, 2):
            height = min(2, count - panel)
            gram = lax.dot_general(
                weighted_ref[:, panel * LANES : (panel + height) * LANES],
                coeffs_ref[where, panel * LANES :],
                (((0,), (0,)), ((), ())),
                preferred_element_type=F32,
            )
            for n, (row, column) in enumerate(blocks_of(aux_count)):
                if not panel <= row < panel + height:
                    continue
                down, across = (row - panel) * LANES, (column - panel) * LANES
                tile = gram[down : down + LANES, across : across + LANES]
                first = jnp.broadcast_to(
                    coulomb[:, row * LANES : (row + 1) * LANES], (LANES, LANES)
                ).T
                second = coulomb[:, column * LANES : (column + 1) * LANES]
                gram_ref[transfer, n] = (first * tile * second).astype(BF16)


def project(occ, virtual, basis, occ_energy, virt_energy, coulomb, scale):
    terms, occ_count, grid_count = occ.shape
    local_k, group_count, _ = virtual.shape
    aux_count = basis.shape[0]
    transfers = terms // local_k
    rows = terms * occ_count * group_count
    blocks = len(blocks_of(aux_count))
    return pl.pallas_call(
        functools.partial(project_kernel, scale=scale),
        in_specs=[VMEM_SPEC] * 5 + [pl.BlockSpec(memory_space=pl.ANY)],
        out_specs=[VMEM_SPEC] * 2,
        out_shape=[
            jax.ShapeDtypeStruct((rows, aux_count), BF16),
            jax.ShapeDtypeStruct((transfers, blocks, LANES, LANES), BF16),
        ],
        scratch_shapes=[
            pltpu.VMEM((rows // transfers, aux_count), BF16),
            pltpu.VMEM(basis.shape, BF16),
            pltpu.VMEM((rows, aux_count), F32),
            pltpu.SemaphoreType.DMA((2,)),
        ],
        compiler_params=pltpu.CompilerParams(vmem_limit_bytes=KERNEL_VMEM),
        cost_estimate=pl.CostEstimate(
            flops=2 * rows * grid_count * aux_count, bytes_accessed=8 << 20, transcendentals=0
        ),
        name="project",
    )(occ, virtual, occ_energy, virt_energy, coulomb, basis)


def screen_coeffs(coeffs_ref, packed_ref, screen_ref, screened_ref):
    transfers = packed_ref.shape[0]
    aux_count = coeffs_ref.shape[1]
    rows = coeffs_ref.shape[0] // transfers
    for transfer in range(transfers):
        for n, (row, column) in enumerate(blocks_of(aux_count)):
            tile = packed_ref[transfer, n]
            upper = slice(row * LANES, (row + 1) * LANES)
            lower = slice(column * LANES, (column + 1) * LANES)
            screen_ref[upper, lower] = tile
            if row != column:
                screen_ref[lower, upper] = tile.T
        where = slice(transfer * rows, (transfer + 1) * rows)
        screened_ref[where, :] = jnp.dot(
            coeffs_ref[where, :], screen_ref[...], preferred_element_type=F32
        ).astype(BF16)


def respond_half(screened_ref, basis_ref, held_ref, sems, occ_ref, virt_ref, outs, half, before=None):
    term_ref, update_ref = outs
    terms, occ_count, _ = occ_ref.shape
    local_k, group_count, _ = virt_ref.shape
    rows = occ_count * group_count
    transfers = terms // local_k
    span = term_ref.shape[2]
    width = min(512, span)

    def grid_of(step):
        return pl.ds(pl.multiple_of(half * span + step * width, width), width)

    def fetch(step):
        return pltpu.make_async_copy(
            basis_ref.at[:, grid_of(step)], held_ref.at[step], sems.at[step]
        )

    for step in range(span // width):
        fetch(step).start()
    if before is not None:
        before()

    def chunk(step, carry):
        to = pl.ds(pl.multiple_of(step * width, width), width)
        grid = grid_of(step)
        fetch(step).wait()
        for k in range(local_k):
            virt = virt_ref[k, :, grid].astype(F32)
            total = None
            for transfer in range(transfers):
                term = transfer * local_k + k
                field = jnp.dot(
                    screened_ref[term * rows : (term + 1) * rows, :],
                    held_ref[step],
                    preferred_element_type=F32,
                ).astype(BF16)
                occ = occ_ref[term, :, grid].astype(F32)
                virt_term = None
                lines = []
                for i in range(occ_count):
                    piece = field[i * group_count : (i + 1) * group_count].astype(F32)
                    lines.append(jnp.sum(piece * virt, axis=0, keepdims=True))
                    product = piece * occ[i : i + 1]
                    virt_term = product if virt_term is None else virt_term + product
                term_ref[term, :, to] = jnp.concatenate(lines, axis=0).astype(BF16)
                virt_term = virt_term.astype(BF16).astype(F32)
                total = virt_term if total is None else total + virt_term
            update_ref[k, :, to] = total.astype(BF16)
        return carry

    lax.fori_loop(0, span // width, chunk, 0)


def respond_far_kernel(
    coeffs_ref, packed_ref, occ_ref, virt_ref, basis_ref,
    term_ref, update_ref, screened_ref, screen_ref, held_ref, sems,
):
    y = (lax.axis_index("band") // 2) % 2
    respond_half(
        screened_ref, basis_ref, held_ref, sems, occ_ref, virt_ref, (term_ref, update_ref), 1 - y,
        lambda: screen_coeffs(coeffs_ref, packed_ref, screen_ref, screened_ref),
    )


def respond_near_kernel(
    screened_ref, occ_ref, virt_ref, basis_ref, term_ref, update_ref, held_ref, sems
):
    y = (lax.axis_index("band") // 2) % 2
    respond_half(
        screened_ref, basis_ref, held_ref, sems, occ_ref, virt_ref, (term_ref, update_ref), y
    )


def respond(coeffs, packed, basis, occ, virtual):
    terms, occ_count, grid_count = occ.shape
    local_k, group_count, _ = virtual.shape
    rows, aux_count = coeffs.shape
    half = grid_count // 2
    width = min(512, half)
    any_spec = pl.BlockSpec(memory_space=pl.ANY)
    shapes = [
        jax.ShapeDtypeStruct((terms, occ_count, half), BF16),
        jax.ShapeDtypeStruct((local_k, group_count, half), BF16),
    ]
    held = [
        pltpu.VMEM((half // width, aux_count, width), BF16),
        pltpu.SemaphoreType.DMA((half // width,)),
    ]
    params = pltpu.CompilerParams(vmem_limit_bytes=KERNEL_VMEM)
    cost = pl.CostEstimate(
        flops=rows * grid_count * aux_count, bytes_accessed=4 << 20, transcendentals=0
    )
    far_terms, far_update, screened = pl.pallas_call(
        respond_far_kernel,
        in_specs=[VMEM_SPEC] * 4 + [any_spec],
        out_specs=[VMEM_SPEC] * 3,
        out_shape=shapes + [jax.ShapeDtypeStruct(coeffs.shape, BF16)],
        scratch_shapes=[pltpu.VMEM((aux_count, aux_count), BF16)] + held,
        compiler_params=params,
        cost_estimate=cost,
        name="respond_far",
    )(coeffs, packed, occ, virtual, basis)
    near_terms, near_update = pl.pallas_call(
        respond_near_kernel,
        in_specs=[VMEM_SPEC] * 3 + [any_spec],
        out_specs=[VMEM_SPEC] * 2,
        out_shape=shapes,
        scratch_shapes=held,
        compiler_params=params,
        cost_estimate=cost,
        name="respond_near",
    )(screened, occ, virtual, basis)
    return (far_terms, near_terms), (far_update, near_update)


def shards(occupied, virtual, occ_energy, virt_energy, partner, coulomb, basis):
    local_k, occ_count, grid_count = occupied.shape
    group_count = virtual.shape[1]
    aux_count = basis.shape[0]
    transfers = partner.shape[0]
    cube = Hypercube()
    total_k = local_k * cube.ka
    virt_count = group_count * cube.band
    gram_scale = 1.0 / math.sqrt(total_k * occ_count * virt_count * aux_count)
    occ_scale = 1.0 / math.sqrt(transfers * virt_count)
    ka = lax.axis_index("ka")

    own_energy = lax.dynamic_slice_in_dim(virt_energy, ka * local_k, local_k, axis=0)
    own_energy = jnp.broadcast_to(own_energy[:, :, None], own_energy.shape + (LANES,))
    sources = partners_of(partner, ka, local_k)
    neighbour_sources = partners_of(partner, jnp.bitwise_xor(ka, 1), local_k)
    partner_occ, partner_energy = fetch_partners(
        cube, occupied, occ_energy, sources, neighbour_sources
    )
    partner_energy = jnp.broadcast_to(
        partner_energy[:, :, None], partner_energy.shape + (LANES,)
    )
    coeffs, packed = project(
        partner_occ, virtual, basis, partner_energy, own_energy, coulomb, gram_scale
    )
    packed = reduce_screen(cube, packed)
    (far_terms, near_terms), (far, near) = respond(coeffs, packed, basis, partner_occ, virtual)
    arrived = cube.swap(far_terms, cube.y)
    terms = (near_terms.astype(F32) + arrived.astype(F32)).astype(BF16)
    occ_total = return_occupied(cube, terms, local_k, sources, neighbour_sources)
    lower = cube.bit(cube.y) == 0
    virt_update = jnp.concatenate(
        [jnp.where(lower, near, far), jnp.where(lower, far, near)], axis=2
    )
    return ((occ_total * occ_scale).astype(BF16), virt_update)


def solution(mesh):
    in_specs = (
        P("ka", None, None),
        P("ka", "band", None),
        P("ka", None),
        P(None, "band"),
        P(),
        P(),
        P(),
    )
    out_specs = (P("ka", None, "band"), P("ka", "band", None))
    return jax.shard_map(shards, mesh=mesh, in_specs=in_specs, out_specs=out_specs, check_vma=False)
```

```python
import functools
import math

import jax
import jax.numpy as jnp
from jax import lax
from jax.experimental import pallas as pl
from jax.experimental.pallas import tpu as pltpu
from jax.sharding import PartitionSpec as P

FREQUENCY = 2.5
BROADENING = 0.4
LANES = 128
KERNEL_VMEM = 48 << 20
VMEM_SPEC = pl.BlockSpec(memory_space=pltpu.VMEM)
BF16 = jnp.bfloat16
F32 = jnp.float32


def response(energy_gaps):
    shifted = FREQUENCY - energy_gaps
    return shifted / (shifted * shifted + BROADENING * BROADENING)


def pick(stack, index):
    return lax.dynamic_index_in_dim(stack, index, 0, keepdims=False)


class Hypercube:
    def __init__(self):
        self.ka = lax.axis_size("ka")
        self.band = lax.axis_size("band")
        self.count = self.ka * self.band
        assert self.band == 4 and self.ka >= 2 and self.ka & (self.ka - 1) == 0
        self.index = lax.axis_index("ka") * self.band + lax.axis_index("band")
        self.core, self.y, self.x = 1, 2, 4
        rest = [bit for bit in (1 << n for n in range(3, 31)) if bit < self.count]
        self.groups = [rest[n : n + 2] for n in range(0, len(rest), 2)]

    def bit(self, mask):
        return (self.index // mask) % 2

    def swap(self, value, mask):
        return lax.ppermute(
            value, ("ka", "band"), [(device, device ^ mask) for device in range(self.count)]
        )


def masks_of(bits):
    return [sum(bit for n, bit in enumerate(bits) if (d >> n) & 1) for d in range(1, 1 << len(bits))]


def sum_scatter(cube, parts, bits):
    me = sum(cube.bit(bit) << n for n, bit in enumerate(bits))
    total = pick(parts, me).astype(F32)
    arrived = [
        cube.swap(pick(parts, jnp.bitwise_xor(me, d + 1)), mask)
        for d, mask in enumerate(masks_of(bits))
    ]
    for term in arrived:
        total = total + term.astype(F32)
    return total


def gather_differences(cube, value, bits):
    return jnp.stack([value] + [cube.swap(value, mask) for mask in masks_of(bits)])


def gather_parts(cube, value, bits):
    me = sum(cube.bit(bit) << n for n, bit in enumerate(bits))
    differences = gather_differences(cube, value, bits)
    return jnp.stack(
        [pick(differences, jnp.bitwise_xor(me, d)) for d in range(1 << len(bits))]
    )


def blocks_of(aux_count):
    count = aux_count // LANES
    return [(row, column) for row in range(count) for column in range(row, count)]


def split_float(value):
    high = lax.reduce_precision(value, 8, 7)
    middle = lax.reduce_precision(value - high, 8, 7)
    low = value - high - middle
    return high.astype(BF16), middle.astype(BF16), low.astype(BF16)


def partners_of(partner, device, local_k):
    every_k = jnp.arange(partner.shape[1], dtype=jnp.int32)
    own_k = device * local_k + jnp.arange(local_k, dtype=jnp.int32)
    here = every_k[None, None, :] == own_k[None, :, None]
    return jnp.sum(jnp.where(here, partner[:, None, :], 0), axis=2).reshape(-1)


def fetch_partners(cube, occupied, occ_energy, sources, neighbour_sources):
    local_k, occ_count, grid_count = occupied.shape
    width = grid_count // 2
    ka = lax.axis_index("ka")
    first = cube.bit(cube.core) == 0
    half = jnp.where(first, occupied[:, :, :width], occupied[:, :, width:])
    pieces = jnp.stack(split_float(occ_energy), axis=2)
    payload = jnp.concatenate(
        [half, jnp.pad(pieces, ((0, 0), (0, 0), (0, LANES - pieces.shape[2])))], axis=2
    )
    gathered = payload[None]
    for bits in cube.groups:
        gathered = gather_differences(cube, gathered, bits).reshape((-1,) + payload.shape)
    gathered = gathered.reshape((-1,) + payload.shape[1:])
    side, upper = ka % 2, ka // 2
    slots = jnp.arange(gathered.shape[0], dtype=jnp.int32)
    held = (jnp.bitwise_xor(slots // local_k, upper) * 2 + side) * local_k + slots % local_k

    def held_of(wanted):
        hits = wanted[:, None] == held[None, :]
        return jnp.sum(
            jnp.where(hits[:, :, None, None], gathered[None].astype(F32), 0.0), axis=1
        ).astype(BF16)

    chosen = held_of(sources) + cube.swap(held_of(neighbour_sources), cube.x)
    mine = jnp.where(first, chosen[:local_k], chosen[local_k:])
    theirs = jnp.where(first, chosen[local_k:], chosen[:local_k])
    energy = mine[:, :, width : width + 3].astype(F32)
    energy = (energy[:, :, 0] + energy[:, :, 1]) + energy[:, :, 2]
    part = mine[:, :, :width]
    other = cube.swap(theirs[:, :, :width], cube.core)
    part = jnp.concatenate([jnp.where(first, part, other), jnp.where(first, other, part)], axis=2)
    return part, energy


def reduce_screen(cube, own):
    rows = own.shape[0] * LANES
    piece = sum_scatter(cube, own.reshape(4, rows // 4, LANES), [cube.y, cube.x]).astype(BF16)
    for bits in cube.groups:
        arrived = [cube.swap(piece, mask) for mask in masks_of(bits)]
        total = piece.astype(F32)
        for term in arrived:
            total = total + term.astype(F32)
        piece = total.astype(BF16)
    return gather_parts(cube, piece, [cube.y, cube.x]).reshape(own.shape)


def return_occupied(cube, part, local_k, sources, neighbour_sources, beside):
    ka = lax.axis_index("ka")
    width = part.shape[2] // 2
    first = cube.bit(cube.core) == 0
    keep = jnp.where(first, part[:, :, :width], part[:, :, width:])
    give = jnp.where(first, part[:, :, width:], part[:, :, :width])
    part = jnp.concatenate([keep, cube.swap(give, cube.core)], axis=0)
    side, upper = ka % 2, ka // 2
    received = cube.swap(part, cube.x)
    both = jnp.concatenate([part, received], axis=0)

    def own_transfer_first(targets):
        turned = jnp.concatenate([targets[local_k:], targets[:local_k]])
        return jnp.where(first, targets, turned)

    targets = jnp.concatenate(
        [own_transfer_first(sources), own_transfer_first(neighbour_sources)]
    )

    def placed(uppers):
        wanted_k = ((uppers * 2 + side) * local_k)[:, None] + jnp.arange(local_k, dtype=jnp.int32)
        hits = targets[None, None, :] == wanted_k[:, :, None]
        return jnp.sum(
            jnp.where(hits[:, :, :, None, None], both[None, None].astype(F32), 0.0), axis=2
        )

    spans = 1
    for bits in cube.groups:
        spans *= 1 << len(bits)
    differences = jnp.arange(spans, dtype=jnp.int32)
    value = placed(jnp.bitwise_xor(differences, upper))
    for bits in reversed(cube.groups):
        size = 1 << len(bits)
        value = value.reshape((size, -1) + value.shape[1:])
        total = value[0]
        arrived = [
            cube.swap(value[d + 1].astype(BF16), mask) for d, mask in enumerate(masks_of(bits))
        ]
        arrived[-1], beside = lax.optimization_barrier((arrived[-1], beside))
        for term in arrived:
            total = total + term.astype(F32)
        value = total
    return value[0], beside


def grid_copies(basis_ref, held_ref, sems, starts):
    ends = starts[1:] + [basis_ref.shape[1]]
    return [
        pltpu.make_async_copy(
            basis_ref.at[:, start:end], held_ref.at[:, start:end], sems.at[n]
        )
        for n, (start, end) in enumerate(zip(starts, ends))
    ]


def project_kernel(
    occ_ref, own_ref, other_ref, occ_energy_ref, levels_ref, coulomb_ref, basis_ref,
    coeffs_ref, gram_ref, weighted_ref, held_ref, total_ref, sems, *, scale, starts,
):
    local_k, occ_count, grid_count = occ_ref.shape
    group_count = own_ref.shape[1]
    aux_count = basis_ref.shape[0]
    rows = occ_count * group_count
    count = aux_count // LANES
    parts = list(zip(starts, starts[1:] + (grid_count,)))
    copies = [
        pltpu.make_async_copy(basis_ref.at[:, start:end], held_ref.at[:, start:end], sems.at[n])
        for n, (start, end) in enumerate(parts)
    ]
    for copy in copies:
        copy.start()
    terms = [(virt_ref, k) for virt_ref in (own_ref, other_ref) for k in range(local_k)]
    for n, (start, end) in enumerate(parts):
        copies[n].wait()
        for term, (virt_ref, k) in enumerate(terms):
            virt = virt_ref[k, :, start:end]
            occ = occ_ref[k, :, start:end]
            pair_rows = jnp.concatenate([occ[i : i + 1] * virt for i in range(occ_count)], axis=0)
            coeffs = lax.dot_general(
                pair_rows,
                held_ref[:, start:end],
                (((1,), (1,)), ((), ())),
                preferred_element_type=F32,
            )
            here = slice(term * rows, (term + 1) * rows)
            if n > 0:
                coeffs = total_ref[here, :] + coeffs
            if n < len(parts) - 1:
                total_ref[here, :] = coeffs
                continue
            coeffs_ref[here, :] = coeffs.astype(BF16)
            coeffs = coeffs.astype(BF16)
            for i in range(occ_count):
                first = i * group_count
                weights = response(levels_ref[term] - occ_energy_ref[k][i : i + 1])
                values = coeffs[first : first + group_count].astype(F32)
                weighted_ref[term * rows + first : term * rows + first + group_count, :] = (
                    jnp.concatenate(
                        [values[:, n * LANES : (n + 1) * LANES] * weights for n in range(count)],
                        axis=1,
                    ).astype(BF16)
                )
    coulomb = coulomb_ref[...] * math.sqrt(scale)
    for panel in range(0, count, 2):
        height = min(2, count - panel)
        gram = lax.dot_general(
            weighted_ref[:, panel * LANES : (panel + height) * LANES],
            coeffs_ref[:, panel * LANES :],
            (((0,), (0,)), ((), ())),
            preferred_element_type=F32,
        )
        for n, (row, column) in enumerate(blocks_of(aux_count)):
            if not panel <= row < panel + height:
                continue
            down, across = (row - panel) * LANES, (column - panel) * LANES
            tile = gram[down : down + LANES, across : across + LANES]
            left = jnp.broadcast_to(coulomb[:, row * LANES : (row + 1) * LANES], (LANES, LANES)).T
            right = coulomb[:, column * LANES : (column + 1) * LANES]
            gram_ref[n] = (left * tile * right).astype(BF16)


def project(occ, own, other, basis, occ_energy, levels, coulomb, scale):
    local_k, occ_count, grid_count = occ.shape
    group_count = own.shape[1]
    aux_count = basis.shape[0]
    rows = 2 * local_k * occ_count * group_count
    blocks = len(blocks_of(aux_count))
    starts = (0, grid_count // 8, 3 * grid_count // 8)
    return pl.pallas_call(
        functools.partial(project_kernel, scale=scale, starts=starts),
        in_specs=[VMEM_SPEC] * 6 + [pl.BlockSpec(memory_space=pl.ANY)],
        out_specs=[VMEM_SPEC] * 2,
        out_shape=[
            jax.ShapeDtypeStruct((rows, aux_count), BF16),
            jax.ShapeDtypeStruct((blocks, LANES, LANES), BF16),
        ],
        scratch_shapes=[
            pltpu.VMEM((rows, aux_count), BF16),
            pltpu.VMEM(basis.shape, BF16),
            pltpu.VMEM((rows, aux_count), F32),
            pltpu.SemaphoreType.DMA((len(starts),)),
        ],
        compiler_params=pltpu.CompilerParams(vmem_limit_bytes=KERNEL_VMEM),
        cost_estimate=pl.CostEstimate(
            flops=2 * rows * grid_count * aux_count, bytes_accessed=8 << 20, transcendentals=0
        ),
        name="project",
    )(occ, own, other, occ_energy, levels, coulomb, basis)


def screen_coeffs(coeffs_ref, packed_ref, screen_ref, screened_ref):
    for n, (row, column) in enumerate(blocks_of(coeffs_ref.shape[1])):
        tile = packed_ref[n]
        upper = slice(row * LANES, (row + 1) * LANES)
        lower = slice(column * LANES, (column + 1) * LANES)
        screen_ref[upper, lower] = tile
        if row != column:
            screen_ref[lower, upper] = tile.T
    screened_ref[...] = jnp.dot(
        coeffs_ref[...], screen_ref[...], preferred_element_type=F32
    ).astype(BF16)


def respond_half(screened_ref, basis_ref, held_ref, sems, inputs, outs, half, before=None):
    occ_ref, own_ref, other_ref = inputs
    term_ref, own_update_ref, other_update_ref = outs
    local_k, occ_count, _ = occ_ref.shape
    group_count = own_ref.shape[1]
    rows = occ_count * group_count
    span = term_ref.shape[2]
    width = held_ref.shape[2]

    def grid_of(step):
        return pl.ds(pl.multiple_of(half * span + step * width, width), width)

    def fetch(step):
        return pltpu.make_async_copy(
            basis_ref.at[:, grid_of(step)], held_ref.at[step], sems.at[step]
        )

    for step in range(span // width):
        fetch(step).start()
    if before is not None:
        before()

    def chunk(step, carry):
        to = pl.ds(pl.multiple_of(step * width, width), width)
        grid = grid_of(step)
        fetch(step).wait()
        for k in range(local_k):
            occ = occ_ref[k, :, grid].astype(F32)
            sums = [None] * occ_count
            sides = ((own_ref, own_update_ref), (other_ref, other_update_ref))
            for side, (virt_ref, update_ref) in enumerate(sides):
                virt = virt_ref[k, :, grid].astype(F32)
                term = side * local_k + k
                field = jnp.dot(
                    screened_ref[term * rows : (term + 1) * rows, :],
                    held_ref[step],
                    preferred_element_type=F32,
                ).astype(BF16)
                virt_term = None
                for i in range(occ_count):
                    piece = field[i * group_count : (i + 1) * group_count].astype(F32)
                    line = jnp.sum((piece * virt).reshape(group_count // 8, 8, width), axis=0)
                    sums[i] = line if side == 0 else sums[i] + line
                    product = piece * occ[i : i + 1]
                    virt_term = product if virt_term is None else virt_term + product
                update_ref[k, :, to] = virt_term.astype(BF16)
            term_ref[k, :, to] = jnp.concatenate(
                [jnp.sum(line, axis=0, keepdims=True) for line in sums], axis=0
            ).astype(BF16)
        return carry

    lax.fori_loop(0, span // width, chunk, 0)


def upper_half():
    return (lax.axis_index("band") // 2) % 2


def respond_far_kernel(
    coeffs_ref, packed_ref, occ_ref, own_ref, other_ref, basis_ref,
    term_ref, own_update_ref, other_update_ref, screened_ref, screen_ref, held_ref, sems,
):
    respond_half(
        screened_ref, basis_ref, held_ref, sems, (occ_ref, own_ref, other_ref),
        (term_ref, own_update_ref, other_update_ref), 1 - upper_half(),
        lambda: screen_coeffs(coeffs_ref, packed_ref, screen_ref, screened_ref),
    )


def respond_near_kernel(
    screened_ref, occ_ref, own_ref, other_ref, basis_ref,
    term_ref, own_update_ref, other_update_ref, held_ref, sems,
):
    respond_half(
        screened_ref, basis_ref, held_ref, sems, (occ_ref, own_ref, other_ref),
        (term_ref, own_update_ref, other_update_ref), upper_half(),
    )


def respond(coeffs, packed, basis, occ, own, other):
    local_k, occ_count, grid_count = occ.shape
    group_count = own.shape[1]
    rows, aux_count = coeffs.shape
    half = grid_count // 2
    width = min(512, half)
    any_spec = pl.BlockSpec(memory_space=pl.ANY)
    shapes = [
        jax.ShapeDtypeStruct((local_k, occ_count, half), BF16),
        jax.ShapeDtypeStruct((local_k, group_count, half), BF16),
        jax.ShapeDtypeStruct((local_k, group_count, half), BF16),
    ]
    held = [
        pltpu.VMEM((half // width, aux_count, width), BF16),
        pltpu.SemaphoreType.DMA((half // width,)),
    ]
    params = pltpu.CompilerParams(vmem_limit_bytes=KERNEL_VMEM)
    cost = pl.CostEstimate(
        flops=rows * grid_count * aux_count, bytes_accessed=4 << 20, transcendentals=0
    )
    *far, screened = pl.pallas_call(
        respond_far_kernel,
        in_specs=[VMEM_SPEC] * 5 + [any_spec],
        out_specs=[VMEM_SPEC] * 4,
        out_shape=shapes + [jax.ShapeDtypeStruct(coeffs.shape, BF16)],
        scratch_shapes=[pltpu.VMEM((aux_count, aux_count), BF16)] + held,
        compiler_params=params,
        cost_estimate=cost,
        name="respond_far",
    )(coeffs, packed, occ, own, other, basis)
    near = pl.pallas_call(
        respond_near_kernel,
        in_specs=[VMEM_SPEC] * 4 + [any_spec],
        out_specs=[VMEM_SPEC] * 3,
        out_shape=shapes,
        scratch_shapes=held,
        compiler_params=params,
        cost_estimate=cost,
        name="respond_near",
    )(screened, occ, own, other, basis)
    return far, near


def shards(occupied, virtual, occ_energy, virt_energy, partner, coulomb, basis):
    local_k, occ_count, grid_count = occupied.shape
    group_count = virtual.shape[1]
    aux_count = basis.shape[0]
    transfers = partner.shape[0]
    assert transfers == 2
    cube = Hypercube()
    total_k = local_k * cube.ka
    virt_count = group_count * cube.band
    gram_scale = 1.0 / math.sqrt(total_k * occ_count * virt_count * aux_count)
    occ_scale = 1.0 / math.sqrt(transfers * virt_count)
    ka = lax.axis_index("ka")

    first = cube.bit(cube.core) == 0
    other_virtual = cube.swap(virtual, cube.core)

    def level_rows(energy):
        rows = lax.dynamic_slice_in_dim(energy, ka * local_k, local_k, axis=0)
        return jnp.broadcast_to(rows[:, :, None], rows.shape + (LANES,))

    levels = jnp.concatenate(
        [level_rows(virt_energy), level_rows(cube.swap(virt_energy, cube.core))]
    )
    sources = partners_of(partner, ka, local_k)
    neighbour_sources = partners_of(partner, jnp.bitwise_xor(ka, 1), local_k)
    partner_occ, partner_energy = fetch_partners(
        cube, occupied, occ_energy, sources, neighbour_sources
    )
    partner_energy = jnp.broadcast_to(
        partner_energy[:, :, None], partner_energy.shape + (LANES,)
    )
    factors = jnp.where(first, coulomb[:1], coulomb[1:])
    coeffs, packed = project(
        partner_occ, virtual, other_virtual, basis, partner_energy, levels, factors, gram_scale
    )
    packed = reduce_screen(cube, packed)
    far, near = respond(coeffs, packed, basis, partner_occ, virtual, other_virtual)
    arrived = cube.swap(far[0], cube.y)
    terms = (near[0].astype(F32) + arrived.astype(F32)).astype(BF16)
    updates = [
        (own.astype(F32) + cube.swap(other, cube.core).astype(F32)).astype(BF16)
        for _, own, other in (far, near)
    ]
    lower = cube.bit(cube.y) == 0
    virt_update = jnp.concatenate(
        [jnp.where(lower, updates[1], updates[0]), jnp.where(lower, updates[0], updates[1])],
        axis=2,
    )
    occ_total, virt_update = return_occupied(
        cube, terms, local_k, sources, neighbour_sources, virt_update
    )
    return ((occ_total * occ_scale).astype(BF16), virt_update)


def solution(mesh):
    in_specs = (
        P("ka", None, None),
        P("ka", "band", None),
        P("ka", None),
        P(None, "band"),
        P(),
        P(),
        P(),
    )
    out_specs = (P("ka", None, "band"), P("ka", "band", None))
    return jax.shard_map(shards, mesh=mesh, in_specs=in_specs, out_specs=out_specs, check_vma=False)
```

```python
import functools
import math

import jax
import jax.numpy as jnp
from jax import lax
from jax.experimental import pallas as pl
from jax.experimental.pallas import tpu as pltpu
from jax.sharding import PartitionSpec as P

FREQUENCY = 2.5
BROADENING = 0.4
LANES = 128
PROJECT_VMEM = 48 << 20
FAR_VMEM = 45 << 20
NEAR_VMEM = 32 << 20
VMEM_SPEC = pl.BlockSpec(memory_space=pltpu.VMEM)
BF16 = jnp.bfloat16
F32 = jnp.float32


def response(energy_gaps):
    shifted = FREQUENCY - energy_gaps
    return shifted / (shifted * shifted + BROADENING * BROADENING)


def pick(stack, index):
    return lax.dynamic_index_in_dim(stack, index, 0, keepdims=False)


class Hypercube:
    def __init__(self):
        self.ka = lax.axis_size("ka")
        self.band = lax.axis_size("band")
        self.count = self.ka * self.band
        assert self.band == 4 and self.ka >= 2 and self.ka & (self.ka - 1) == 0
        self.index = lax.axis_index("ka") * self.band + lax.axis_index("band")
        self.core, self.y, self.x = 1, 2, 4
        rest = [bit for bit in (1 << n for n in range(3, 31)) if bit < self.count]
        self.groups = [rest[n : n + 2] for n in range(0, len(rest), 2)]

    def bit(self, mask):
        return (self.index // mask) % 2

    def swap(self, value, mask):
        return lax.ppermute(
            value, ("ka", "band"), [(device, device ^ mask) for device in range(self.count)]
        )


def masks_of(bits):
    return [sum(bit for n, bit in enumerate(bits) if (d >> n) & 1) for d in range(1, 1 << len(bits))]


def sum_scatter(cube, parts, bits):
    me = sum(cube.bit(bit) << n for n, bit in enumerate(bits))
    total = pick(parts, me).astype(F32)
    arrived = [
        cube.swap(pick(parts, jnp.bitwise_xor(me, d + 1)), mask)
        for d, mask in enumerate(masks_of(bits))
    ]
    for term in arrived:
        total = total + term.astype(F32)
    return total


def gather_differences(cube, value, bits):
    return jnp.stack([value] + [cube.swap(value, mask) for mask in masks_of(bits)])


def gather_parts(cube, value, bits):
    me = sum(cube.bit(bit) << n for n, bit in enumerate(bits))
    differences = gather_differences(cube, value, bits)
    return jnp.stack(
        [pick(differences, jnp.bitwise_xor(me, d)) for d in range(1 << len(bits))]
    )


def blocks_of(aux_count):
    count = aux_count // LANES
    return [(row, column) for row in range(count) for column in range(row, count)]


def split_float(value):
    high = lax.reduce_precision(value, 8, 7)
    middle = lax.reduce_precision(value - high, 8, 7)
    low = value - high - middle
    return high.astype(BF16), middle.astype(BF16), low.astype(BF16)


def partners_of(partner, device, local_k):
    every_k = jnp.arange(partner.shape[1], dtype=jnp.int32)
    own_k = device * local_k + jnp.arange(local_k, dtype=jnp.int32)
    here = every_k[None, None, :] == own_k[None, :, None]
    return jnp.sum(jnp.where(here, partner[:, None, :], 0), axis=2).reshape(-1)


def fetch_partners(cube, occupied, occ_energy, sources, neighbour_sources, beside):
    local_k, occ_count, grid_count = occupied.shape
    width = grid_count // 2
    ka = lax.axis_index("ka")
    first = cube.bit(cube.core) == 0
    half = jnp.where(first, occupied[:, :, :width], occupied[:, :, width:])
    pieces = jnp.stack(split_float(occ_energy), axis=2)
    payload = jnp.concatenate(
        [half, jnp.pad(pieces, ((0, 0), (0, 0), (0, LANES - pieces.shape[2])))], axis=2
    )
    gathered = payload[None]
    for bits in cube.groups:
        gathered = gather_differences(cube, gathered, bits).reshape((-1,) + payload.shape)
    gathered = gathered.reshape((-1,) + payload.shape[1:])
    side, upper = ka % 2, ka // 2
    slots = jnp.arange(gathered.shape[0], dtype=jnp.int32)
    held = (jnp.bitwise_xor(slots // local_k, upper) * 2 + side) * local_k + slots % local_k

    def held_of(wanted):
        hits = wanted[:, None] == held[None, :]
        return jnp.sum(
            jnp.where(hits[:, :, None, None], gathered[None].astype(F32), 0.0), axis=1
        ).astype(BF16)

    received = cube.swap(held_of(neighbour_sources), cube.x)
    received, beside = lax.optimization_barrier((received, beside))
    chosen = held_of(sources) + received
    mine = jnp.where(first, chosen[:local_k], chosen[local_k:])
    theirs = jnp.where(first, chosen[local_k:], chosen[:local_k])
    energy = mine[:, :, width : width + 3].astype(F32)
    energy = (energy[:, :, 0] + energy[:, :, 1]) + energy[:, :, 2]
    part = mine[:, :, :width]
    other = cube.swap(theirs[:, :, :width], cube.core)
    part = jnp.concatenate([jnp.where(first, part, other), jnp.where(first, other, part)], axis=2)
    return part, energy, beside


def reduce_screen(cube, own):
    rows = own.shape[0] * LANES
    piece = sum_scatter(cube, own.reshape(4, rows // 4, LANES), [cube.y, cube.x]).astype(BF16)
    for bits in cube.groups:
        arrived = [cube.swap(piece, mask) for mask in masks_of(bits)]
        total = piece.astype(F32)
        for term in arrived:
            total = total + term.astype(F32)
        piece = total.astype(BF16)
    return gather_parts(cube, piece, [cube.y, cube.x]).reshape(own.shape)


def return_occupied(cube, part, local_k, sources, neighbour_sources, beside):
    ka = lax.axis_index("ka")
    width = part.shape[2] // 2
    first = cube.bit(cube.core) == 0
    keep = jnp.where(first, part[:, :, :width], part[:, :, width:])
    give = jnp.where(first, part[:, :, width:], part[:, :, :width])
    part = jnp.concatenate([keep, cube.swap(give, cube.core)], axis=0)
    side, upper = ka % 2, ka // 2
    received = cube.swap(part, cube.x)
    both = jnp.concatenate([part, received], axis=0)

    def own_transfer_first(targets):
        turned = jnp.concatenate([targets[local_k:], targets[:local_k]])
        return jnp.where(first, targets, turned)

    targets = jnp.concatenate(
        [own_transfer_first(sources), own_transfer_first(neighbour_sources)]
    )

    def placed(uppers):
        wanted_k = ((uppers * 2 + side) * local_k)[:, None] + jnp.arange(local_k, dtype=jnp.int32)
        hits = targets[None, None, :] == wanted_k[:, :, None]
        return jnp.sum(
            jnp.where(hits[:, :, :, None, None], both[None, None].astype(F32), 0.0), axis=2
        )

    spans = 1
    for bits in cube.groups:
        spans *= 1 << len(bits)
    differences = jnp.arange(spans, dtype=jnp.int32)
    value = placed(jnp.bitwise_xor(differences, upper))
    for bits in reversed(cube.groups):
        size = 1 << len(bits)
        value = value.reshape((size, -1) + value.shape[1:])
        total = value[0]
        arrived = [
            cube.swap(value[d + 1].astype(BF16), mask) for d, mask in enumerate(masks_of(bits))
        ]
        arrived[-1], beside = lax.optimization_barrier((arrived[-1], beside))
        for term in arrived:
            total = total + term.astype(F32)
        value = total
    return value[0], beside


def grid_copies(basis_ref, held_ref, sems, starts):
    ends = starts[1:] + [basis_ref.shape[1]]
    return [
        pltpu.make_async_copy(
            basis_ref.at[:, start:end], held_ref.at[:, start:end], sems.at[n]
        )
        for n, (start, end) in enumerate(zip(starts, ends))
    ]


def project_kernel(
    occ_ref, own_ref, other_ref, occ_energy_ref, levels_ref, coulomb_ref, first_ref, basis_ref,
    coeffs_ref, gram_ref, weighted_ref, held_ref, total_ref, sems, *, scale, starts,
):
    local_k, occ_count, grid_count = occ_ref.shape
    group_count = own_ref.shape[1]
    aux_count = basis_ref.shape[0]
    rows = occ_count * group_count
    count = aux_count // LANES
    parts = list(zip(starts, starts[1:] + (grid_count,)))
    offset = starts[1]
    copies = [None] + [
        pltpu.make_async_copy(
            basis_ref.at[:, start:end],
            held_ref.at[:, start - offset : end - offset],
            sems.at[n],
        )
        for n, (start, end) in enumerate(parts[1:])
    ]
    for copy in copies[1:]:
        copy.start()
    terms = [(virt_ref, k) for virt_ref in (own_ref, other_ref) for k in range(local_k)]
    for n, (start, end) in enumerate(parts):
        if n > 0:
            copies[n].wait()
        for term, (virt_ref, k) in enumerate(terms):
            virt = virt_ref[k, :, start:end]
            occ = occ_ref[k, :, start:end]
            pair_rows = jnp.concatenate([occ[i : i + 1] * virt for i in range(occ_count)], axis=0)
            coeffs = lax.dot_general(
                pair_rows,
                held_ref[:, start - offset : end - offset] if n > 0 else first_ref[...],
                (((1,), (1,)), ((), ())),
                preferred_element_type=F32,
            )
            here = slice(term * rows, (term + 1) * rows)
            if n > 0:
                coeffs = total_ref[here, :] + coeffs
            if n < len(parts) - 1:
                total_ref[here, :] = coeffs
                continue
            coeffs_ref[here, :] = coeffs.astype(BF16)
            coeffs = coeffs.astype(BF16)
            for i in range(occ_count):
                first = i * group_count
                weights = response(levels_ref[term] - occ_energy_ref[k][i : i + 1])
                values = coeffs[first : first + group_count].astype(F32)
                weighted_ref[term * rows + first : term * rows + first + group_count, :] = (
                    jnp.concatenate(
                        [values[:, n * LANES : (n + 1) * LANES] * weights for n in range(count)],
                        axis=1,
                    ).astype(BF16)
                )
    coulomb = coulomb_ref[...] * math.sqrt(scale)
    for panel in range(0, count, 2):
        height = min(2, count - panel)
        gram = lax.dot_general(
            weighted_ref[:, panel * LANES : (panel + height) * LANES],
            coeffs_ref[:, panel * LANES :],
            (((0,), (0,)), ((), ())),
            preferred_element_type=F32,
        )
        for n, (row, column) in enumerate(blocks_of(aux_count)):
            if not panel <= row < panel + height:
                continue
            down, across = (row - panel) * LANES, (column - panel) * LANES
            tile = gram[down : down + LANES, across : across + LANES]
            left = jnp.broadcast_to(coulomb[:, row * LANES : (row + 1) * LANES], (LANES, LANES)).T
            right = coulomb[:, column * LANES : (column + 1) * LANES]
            gram_ref[n] = (left * tile * right).astype(BF16)


def project(occ, own, other, first, basis, occ_energy, levels, coulomb, scale):
    local_k, occ_count, grid_count = occ.shape
    group_count = own.shape[1]
    aux_count = basis.shape[0]
    rows = 2 * local_k * occ_count * group_count
    blocks = len(blocks_of(aux_count))
    starts = (0, first.shape[1], 3 * first.shape[1])
    return pl.pallas_call(
        functools.partial(project_kernel, scale=scale, starts=starts),
        in_specs=[VMEM_SPEC] * 7 + [pl.BlockSpec(memory_space=pl.ANY)],
        out_specs=[VMEM_SPEC] * 2,
        out_shape=[
            jax.ShapeDtypeStruct((rows, aux_count), BF16),
            jax.ShapeDtypeStruct((blocks, LANES, LANES), BF16),
        ],
        scratch_shapes=[
            pltpu.VMEM((rows, aux_count), BF16),
            pltpu.VMEM((aux_count, grid_count - starts[1]), BF16),
            pltpu.VMEM((rows, aux_count), F32),
            pltpu.SemaphoreType.DMA((len(starts) - 1,)),
        ],
        compiler_params=pltpu.CompilerParams(vmem_limit_bytes=PROJECT_VMEM),
        cost_estimate=pl.CostEstimate(
            flops=2 * rows * grid_count * aux_count, bytes_accessed=8 << 20, transcendentals=0
        ),
        name="project",
    )(occ, own, other, occ_energy, levels, coulomb, first, basis)


def screen_coeffs(coeffs_ref, packed_ref, screen_ref, screened_ref):
    for n, (row, column) in enumerate(blocks_of(coeffs_ref.shape[1])):
        tile = packed_ref[n]
        upper = slice(row * LANES, (row + 1) * LANES)
        lower = slice(column * LANES, (column + 1) * LANES)
        screen_ref[upper, lower] = tile
        if row != column:
            screen_ref[lower, upper] = tile.T
    screened_ref[...] = jnp.dot(
        coeffs_ref[...], screen_ref[...], preferred_element_type=F32
    ).astype(BF16)


def respond_half(screened_ref, held_ref, field_ref, inputs, outs, half, arrived=None):
    occ_ref, own_ref, other_ref = inputs
    term_ref, own_update_ref, other_update_ref = outs
    local_k, occ_count, _ = occ_ref.shape
    group_count = own_ref.shape[1]
    rows = occ_count * group_count
    span = term_ref.shape[2]
    width = held_ref.shape[2]

    def grid_of(step):
        return pl.ds(pl.multiple_of(half * span + step * width, width), width)

    def chunk(step, carry):
        to = pl.ds(pl.multiple_of(step * width, width), width)
        grid = grid_of(step)
        if arrived is not None:
            arrived(step)
        field_ref[...] = jnp.dot(
            screened_ref[...], held_ref[step], preferred_element_type=F32
        ).astype(BF16)
        for k in range(local_k):
            occ = occ_ref[k, :, grid].astype(F32)
            sums = [None] * occ_count
            sides = ((own_ref, own_update_ref), (other_ref, other_update_ref))
            for side, (virt_ref, update_ref) in enumerate(sides):
                virt = virt_ref[k, :, grid].astype(F32)
                first = (side * local_k + k) * rows
                virt_term = None
                for i in range(occ_count):
                    here = slice(first + i * group_count, first + (i + 1) * group_count)
                    piece = field_ref[here, :].astype(F32)
                    line = jnp.sum((piece * virt).reshape(group_count // 8, 8, width), axis=0)
                    sums[i] = line if side == 0 else sums[i] + line
                    product = piece * occ[i : i + 1]
                    virt_term = product if virt_term is None else virt_term + product
                update_ref[k, :, to] = virt_term.astype(BF16)
            term_ref[k, :, to] = jnp.concatenate(
                [jnp.sum(line, axis=0, keepdims=True) for line in sums], axis=0
            ).astype(BF16)
        return carry

    lax.fori_loop(0, span // width, chunk, 0)


def upper_half():
    return (lax.axis_index("band") // 2) % 2


def respond_far_kernel(
    coeffs_ref, packed_ref, occ_ref, own_ref, other_ref, basis_ref,
    term_ref, own_update_ref, other_update_ref, screened_ref, near_ref,
    screen_ref, far_ref, field_ref, far_sems, near_sem,
):
    steps, _, width = far_ref.shape
    far, near = 1 - upper_half(), upper_half()

    def fetch(half, step, held_ref, sem):
        start = pl.multiple_of((half * steps + step) * width, width)
        return pltpu.make_async_copy(
            basis_ref.at[:, pl.ds(start, width)], held_ref.at[step], sem
        )

    for step in range(steps):
        fetch(far, step, far_ref, far_sems.at[step]).start()
    for step in range(steps):
        fetch(near, step, near_ref, near_sem.at[step]).start()
    screen_coeffs(coeffs_ref, packed_ref, screen_ref, screened_ref)
    respond_half(
        screened_ref, far_ref, field_ref, (occ_ref, own_ref, other_ref),
        (term_ref, own_update_ref, other_update_ref), far,
        lambda step: fetch(far, step, far_ref, far_sems.at[step]).wait(),
    )
    for step in range(steps):
        fetch(near, step, near_ref, near_sem.at[step]).wait()


def respond_near_kernel(
    screened_ref, occ_ref, own_ref, other_ref, near_ref,
    term_ref, own_update_ref, other_update_ref, field_ref,
):
    respond_half(
        screened_ref, near_ref, field_ref, (occ_ref, own_ref, other_ref),
        (term_ref, own_update_ref, other_update_ref), upper_half(),
    )


def respond(coeffs, packed, basis, occ, own, other):
    local_k, occ_count, grid_count = occ.shape
    group_count = own.shape[1]
    rows, aux_count = coeffs.shape
    half = grid_count // 2
    width = min(1024, half)
    any_spec = pl.BlockSpec(memory_space=pl.ANY)
    shapes = [
        jax.ShapeDtypeStruct((local_k, occ_count, half), BF16),
        jax.ShapeDtypeStruct((local_k, group_count, half), BF16),
        jax.ShapeDtypeStruct((local_k, group_count, half), BF16),
    ]
    held = (half // width, aux_count, width)
    cost = pl.CostEstimate(
        flops=rows * grid_count * aux_count, bytes_accessed=4 << 20, transcendentals=0
    )
    *far, screened, near_basis = pl.pallas_call(
        respond_far_kernel,
        in_specs=[VMEM_SPEC] * 5 + [any_spec],
        out_specs=[VMEM_SPEC] * 5,
        out_shape=shapes
        + [jax.ShapeDtypeStruct(coeffs.shape, BF16), jax.ShapeDtypeStruct(held, BF16)],
        scratch_shapes=[
            pltpu.VMEM((aux_count, aux_count), BF16),
            pltpu.VMEM(held, BF16),
            pltpu.VMEM((rows, width), BF16),
            pltpu.SemaphoreType.DMA((held[0],)),
            pltpu.SemaphoreType.DMA((held[0],)),
        ],
        compiler_params=pltpu.CompilerParams(vmem_limit_bytes=FAR_VMEM),
        cost_estimate=cost,
        name="respond_far",
    )(coeffs, packed, occ, own, other, basis)
    near = pl.pallas_call(
        respond_near_kernel,
        in_specs=[VMEM_SPEC] * 5,
        out_specs=[VMEM_SPEC] * 3,
        out_shape=shapes,
        scratch_shapes=[pltpu.VMEM((rows, width), BF16)],
        compiler_params=pltpu.CompilerParams(vmem_limit_bytes=NEAR_VMEM),
        cost_estimate=cost,
        name="respond_near",
    )(screened, occ, own, other, near_basis)
    return far, near


def shards(occupied, virtual, occ_energy, virt_energy, partner, coulomb, basis):
    local_k, occ_count, grid_count = occupied.shape
    group_count = virtual.shape[1]
    aux_count = basis.shape[0]
    transfers = partner.shape[0]
    assert transfers == 2
    cube = Hypercube()
    total_k = local_k * cube.ka
    virt_count = group_count * cube.band
    gram_scale = 1.0 / math.sqrt(total_k * occ_count * virt_count * aux_count)
    occ_scale = 1.0 / math.sqrt(transfers * virt_count)
    ka = lax.axis_index("ka")

    first = cube.bit(cube.core) == 0
    other_virtual = cube.swap(virtual, cube.core)

    def level_rows(energy):
        rows = lax.dynamic_slice_in_dim(energy, ka * local_k, local_k, axis=0)
        return jnp.broadcast_to(rows[:, :, None], rows.shape + (LANES,))

    levels = jnp.concatenate(
        [level_rows(virt_energy), level_rows(cube.swap(virt_energy, cube.core))]
    )
    sources = partners_of(partner, ka, local_k)
    neighbour_sources = partners_of(partner, jnp.bitwise_xor(ka, 1), local_k)
    partner_occ, partner_energy, first_basis = fetch_partners(
        cube, occupied, occ_energy, sources, neighbour_sources, basis[:, : grid_count // 8]
    )
    partner_energy = jnp.broadcast_to(
        partner_energy[:, :, None], partner_energy.shape + (LANES,)
    )
    factors = jnp.where(first, coulomb[:1], coulomb[1:])
    coeffs, packed = project(
        partner_occ, virtual, other_virtual, first_basis, basis, partner_energy, levels, factors,
        gram_scale,
    )
    packed = reduce_screen(cube, packed)
    far, near = respond(coeffs, packed, basis, partner_occ, virtual, other_virtual)
    arrived = cube.swap(far[0], cube.y)
    terms = (near[0].astype(F32) + arrived.astype(F32)).astype(BF16)
    updates = [
        (own.astype(F32) + cube.swap(other, cube.core).astype(F32)).astype(BF16)
        for _, own, other in (far, near)
    ]
    lower = cube.bit(cube.y) == 0
    virt_update = jnp.concatenate(
        [jnp.where(lower, updates[1], updates[0]), jnp.where(lower, updates[0], updates[1])],
        axis=2,
    )
    occ_total, virt_update = return_occupied(
        cube, terms, local_k, sources, neighbour_sources, virt_update
    )
    return ((occ_total * occ_scale).astype(BF16), virt_update)


def solution(mesh):
    in_specs = (
        P("ka", None, None),
        P("ka", "band", None),
        P("ka", None),
        P(None, "band"),
        P(),
        P(),
        P(),
    )
    out_specs = (P("ka", None, "band"), P("ka", "band", None))
    return jax.shard_map(shards, mesh=mesh, in_specs=in_specs, out_specs=out_specs, check_vma=False)
```

```python
import functools
import math

import jax
import jax.numpy as jnp
from jax import lax
from jax.experimental import pallas as pl
from jax.experimental.pallas import tpu as pltpu
from jax.sharding import PartitionSpec as P

FREQUENCY = 2.5
BROADENING = 0.4
LANES = 128
PROJECT_VMEM = 48 << 20
FAR_VMEM = 45 << 20
NEAR_VMEM = 32 << 20
VMEM_SPEC = pl.BlockSpec(memory_space=pltpu.VMEM)
BF16 = jnp.bfloat16
F32 = jnp.float32


def response(energy_gaps):
    shifted = FREQUENCY - energy_gaps
    return shifted / (shifted * shifted + BROADENING * BROADENING)


def pick(stack, index):
    return lax.dynamic_index_in_dim(stack, index, 0, keepdims=False)


class Hypercube:
    def __init__(self):
        self.ka = lax.axis_size("ka")
        self.band = lax.axis_size("band")
        self.count = self.ka * self.band
        assert self.band == 4 and self.ka >= 2 and self.ka & (self.ka - 1) == 0
        self.index = lax.axis_index("ka") * self.band + lax.axis_index("band")
        self.core, self.y, self.x = 1, 2, 4
        rest = [bit for bit in (1 << n for n in range(3, 31)) if bit < self.count]
        self.groups = [rest[n : n + 2] for n in range(0, len(rest), 2)]

    def bit(self, mask):
        return (self.index // mask) % 2

    def swap(self, value, mask):
        return lax.ppermute(
            value, ("ka", "band"), [(device, device ^ mask) for device in range(self.count)]
        )


def masks_of(bits):
    return [sum(bit for n, bit in enumerate(bits) if (d >> n) & 1) for d in range(1, 1 << len(bits))]


def sum_scatter(cube, parts, bits):
    me = sum(cube.bit(bit) << n for n, bit in enumerate(bits))
    total = pick(parts, me).astype(F32)
    arrived = [
        cube.swap(pick(parts, jnp.bitwise_xor(me, d + 1)), mask)
        for d, mask in enumerate(masks_of(bits))
    ]
    for term in arrived:
        total = total + term.astype(F32)
    return total


def gather_differences(cube, value, bits):
    return jnp.stack([value] + [cube.swap(value, mask) for mask in masks_of(bits)])


def gather_parts(cube, value, bits):
    me = sum(cube.bit(bit) << n for n, bit in enumerate(bits))
    differences = gather_differences(cube, value, bits)
    return jnp.stack(
        [pick(differences, jnp.bitwise_xor(me, d)) for d in range(1 << len(bits))]
    )


def blocks_of(aux_count):
    count = aux_count // LANES
    return [(row, column) for row in range(count) for column in range(row + 1, count)]


def packed_rows(aux_count):
    count = aux_count // LANES
    assert count % 2 == 0
    blocks = (len(blocks_of(aux_count)) + count // 2) * LANES
    return blocks, blocks + 64


def split_float(value):
    high = lax.reduce_precision(value, 8, 7)
    middle = lax.reduce_precision(value - high, 8, 7)
    low = value - high - middle
    return high.astype(BF16), middle.astype(BF16), low.astype(BF16)


def partners_of(partner, device, local_k):
    every_k = jnp.arange(partner.shape[1], dtype=jnp.int32)
    own_k = device * local_k + jnp.arange(local_k, dtype=jnp.int32)
    here = every_k[None, None, :] == own_k[None, :, None]
    return jnp.sum(jnp.where(here, partner[:, None, :], 0), axis=2).reshape(-1)


def own_transfer_first(cube, values, local_k):
    first = cube.bit(cube.core) == 0
    low, high = values[:local_k], values[local_k:]
    return jnp.where(first, low, high), jnp.where(first, high, low)


def fetch_partners(cube, occupied, occ_energy, sources, neighbour_sources, beside):
    local_k, occ_count, grid_count = occupied.shape
    width = grid_count // 2
    ka = lax.axis_index("ka")
    first = cube.bit(cube.core) == 0
    half = jnp.where(first, occupied[:, :, :width], occupied[:, :, width:])
    pieces = jnp.stack(split_float(occ_energy), axis=2)
    payload = jnp.concatenate(
        [half, jnp.pad(pieces, ((0, 0), (0, 0), (0, LANES - pieces.shape[2])))], axis=2
    )
    gathered = payload[None]
    for bits in cube.groups:
        gathered = gather_differences(cube, gathered, bits).reshape((-1,) + payload.shape)
    gathered = gathered.reshape((-1,) + payload.shape[1:])
    side, upper = ka % 2, ka // 2
    slots = jnp.arange(gathered.shape[0], dtype=jnp.int32)
    held = (jnp.bitwise_xor(slots // local_k, upper) * 2 + side) * local_k + slots % local_k

    def held_of(wanted):
        hits = wanted[:, None] == held[None, :]
        return jnp.sum(
            jnp.where(hits[:, :, None, None], gathered[None].astype(F32), 0.0), axis=1
        ).astype(BF16)

    own_sources, other_sources = own_transfer_first(cube, sources, local_k)
    own_neighbour, other_neighbour = own_transfer_first(cube, neighbour_sources, local_k)
    along_x = cube.swap(held_of(own_neighbour), cube.x)
    across = cube.swap(held_of(other_neighbour)[:, :, :width], cube.x | cube.core)
    beside_core = cube.swap(held_of(other_sources)[:, :, :width], cube.core)
    along_x, beside = lax.optimization_barrier((along_x, beside))
    mine = held_of(own_sources) + along_x
    other = beside_core + across
    energy = mine[:, :, width : width + 3].astype(F32)
    energy = (energy[:, :, 0] + energy[:, :, 1]) + energy[:, :, 2]
    part = mine[:, :, :width]
    part = jnp.concatenate([jnp.where(first, part, other), jnp.where(first, other, part)], axis=2)
    return part, energy, beside


def reduce_screen(cube, own):
    rows = own.shape[0]
    piece = sum_scatter(cube, own.reshape(4, rows // 4, LANES), [cube.y, cube.x]).astype(BF16)
    for bits in cube.groups:
        arrived = [cube.swap(piece, mask) for mask in masks_of(bits)]
        total = piece.astype(F32)
        for term in arrived:
            total = total + term.astype(F32)
        piece = total.astype(BF16)
    return gather_parts(cube, piece, [cube.y, cube.x]).reshape(own.shape)


def return_occupied(cube, part, local_k, sources, neighbour_sources, beside):
    ka = lax.axis_index("ka")
    width = part.shape[2] // 2
    first = cube.bit(cube.core) == 0
    keep = jnp.where(first, part[:, :, :width], part[:, :, width:])
    give = jnp.where(first, part[:, :, width:], part[:, :, :width])
    along_x = cube.swap(keep, cube.x)
    across = cube.swap(give, cube.x | cube.core)
    beside_core = cube.swap(give, cube.core)
    side, upper = ka % 2, ka // 2
    both = jnp.concatenate([keep, beside_core, along_x, across], axis=0)
    targets = jnp.concatenate(
        own_transfer_first(cube, sources, local_k)
        + own_transfer_first(cube, neighbour_sources, local_k)
    )

    def placed(uppers):
        wanted_k = ((uppers * 2 + side) * local_k)[:, None] + jnp.arange(local_k, dtype=jnp.int32)
        hits = targets[None, None, :] == wanted_k[:, :, None]
        return jnp.sum(
            jnp.where(hits[:, :, :, None, None], both[None, None].astype(F32), 0.0), axis=2
        )

    spans = 1
    for bits in cube.groups:
        spans *= 1 << len(bits)
    differences = jnp.arange(spans, dtype=jnp.int32)
    value = placed(jnp.bitwise_xor(differences, upper))
    for bits in reversed(cube.groups):
        size = 1 << len(bits)
        value = value.reshape((size, -1) + value.shape[1:])
        total = value[0]
        arrived = [
            cube.swap(value[d + 1].astype(BF16), mask) for d, mask in enumerate(masks_of(bits))
        ]
        arrived[-1], beside = lax.optimization_barrier((arrived[-1], beside))
        for term in arrived:
            total = total + term.astype(F32)
        value = total
    return value[0], beside


def grid_copies(basis_ref, held_ref, sems, starts):
    ends = starts[1:] + [basis_ref.shape[1]]
    return [
        pltpu.make_async_copy(
            basis_ref.at[:, start:end], held_ref.at[:, start:end], sems.at[n]
        )
        for n, (start, end) in enumerate(zip(starts, ends))
    ]


def project_kernel(
    occ_ref, own_ref, other_ref, occ_energy_ref, levels_ref, coulomb_ref, first_ref, basis_ref,
    coeffs_ref, gram_ref, weighted_ref, held_ref, total_ref, sems, *, scale, starts,
):
    local_k, occ_count, grid_count = occ_ref.shape
    group_count = own_ref.shape[1]
    aux_count = basis_ref.shape[0]
    rows = occ_count * group_count
    count = aux_count // LANES
    parts = list(zip(starts, starts[1:] + (grid_count,)))
    offset = starts[1]
    copies = [None] + [
        pltpu.make_async_copy(
            basis_ref.at[:, start:end],
            held_ref.at[:, start - offset : end - offset],
            sems.at[n],
        )
        for n, (start, end) in enumerate(parts[1:])
    ]
    for copy in copies[1:]:
        copy.start()
    terms = [(virt_ref, k) for virt_ref in (own_ref, other_ref) for k in range(local_k)]
    for n, (start, end) in enumerate(parts):
        if n > 0:
            copies[n].wait()
        for term, (virt_ref, k) in enumerate(terms):
            virt = virt_ref[k, :, start:end]
            occ = occ_ref[k, :, start:end]
            pair_rows = jnp.concatenate([occ[i : i + 1] * virt for i in range(occ_count)], axis=0)
            coeffs = lax.dot_general(
                pair_rows,
                held_ref[:, start - offset : end - offset] if n > 0 else first_ref[...],
                (((1,), (1,)), ((), ())),
                preferred_element_type=F32,
            )
            here = slice(term * rows, (term + 1) * rows)
            if n > 0:
                coeffs = total_ref[here, :] + coeffs
            if n < len(parts) - 1:
                total_ref[here, :] = coeffs
                continue
            coeffs_ref[here, :] = coeffs.astype(BF16)
            coeffs = coeffs.astype(BF16)
            for i in range(occ_count):
                first = i * group_count
                weights = response(levels_ref[term] - occ_energy_ref[k][i : i + 1])
                values = coeffs[first : first + group_count].astype(F32)
                weighted_ref[term * rows + first : term * rows + first + group_count, :] = (
                    jnp.concatenate(
                        [values[:, n * LANES : (n + 1) * LANES] * weights for n in range(count)],
                        axis=1,
                    ).astype(BF16)
                )
    coulomb = coulomb_ref[...] * math.sqrt(scale)
    tiles = {}
    for panel in range(0, count, 2):
        gram = lax.dot_general(
            weighted_ref[:, panel * LANES : (panel + 2) * LANES],
            coeffs_ref[:, panel * LANES :],
            (((0,), (0,)), ((), ())),
            preferred_element_type=F32,
        )
        for row in (panel, panel + 1):
            left = jnp.broadcast_to(coulomb[:, row * LANES : (row + 1) * LANES], (LANES, LANES)).T
            for column in range(row, count):
                down, across = (row - panel) * LANES, (column - panel) * LANES
                right = coulomb[:, column * LANES : (column + 1) * LANES]
                tiles[row, column] = (
                    left * gram[down : down + LANES, across : across + LANES] * right
                )
    places = blocks_of(aux_count)
    for n, place in enumerate(places):
        gram_ref[n * LANES : (n + 1) * LANES, :] = tiles[place].astype(BF16)
    down = lax.broadcasted_iota(jnp.int32, (LANES, LANES), 0)
    across = lax.broadcasted_iota(jnp.int32, (LANES, LANES), 1)
    lines = []
    for pair in range(count // 2):
        upper, lower = tiles[2 * pair, 2 * pair], tiles[2 * pair + 1, 2 * pair + 1]
        n = len(places) + pair
        gram_ref[n * LANES : (n + 1) * LANES, :] = jnp.where(across >= down, upper, lower).astype(
            BF16
        )
        lines.append(jnp.sum(jnp.where(across == down, lower, 0.0), axis=0, keepdims=True))
    blocks, total_rows = packed_rows(aux_count)
    lines.append(jnp.zeros((total_rows - blocks - len(lines), LANES), F32))
    gram_ref[blocks:, :] = jnp.concatenate(lines, axis=0).astype(BF16)


def project(occ, own, other, first, basis, occ_energy, levels, coulomb, scale):
    local_k, occ_count, grid_count = occ.shape
    group_count = own.shape[1]
    aux_count = basis.shape[0]
    rows = 2 * local_k * occ_count * group_count
    starts = (0, first.shape[1], 3 * first.shape[1])
    return pl.pallas_call(
        functools.partial(project_kernel, scale=scale, starts=starts),
        in_specs=[VMEM_SPEC] * 7 + [pl.BlockSpec(memory_space=pl.ANY)],
        out_specs=[VMEM_SPEC] * 2,
        out_shape=[
            jax.ShapeDtypeStruct((rows, aux_count), BF16),
            jax.ShapeDtypeStruct((packed_rows(aux_count)[1], LANES), BF16),
        ],
        scratch_shapes=[
            pltpu.VMEM((rows, aux_count), BF16),
            pltpu.VMEM((aux_count, grid_count - starts[1]), BF16),
            pltpu.VMEM((rows, aux_count), F32),
            pltpu.SemaphoreType.DMA((len(starts) - 1,)),
        ],
        compiler_params=pltpu.CompilerParams(vmem_limit_bytes=PROJECT_VMEM),
        cost_estimate=pl.CostEstimate(
            flops=2 * rows * grid_count * aux_count, bytes_accessed=8 << 20, transcendentals=0
        ),
        name="project",
    )(occ, own, other, occ_energy, levels, coulomb, first, basis)


def screen_coeffs(coeffs_ref, packed_ref, screen_ref, screened_ref):
    aux_count = coeffs_ref.shape[1]
    places = blocks_of(aux_count)
    for n, (row, column) in enumerate(places):
        tile = packed_ref[n * LANES : (n + 1) * LANES, :]
        upper = slice(row * LANES, (row + 1) * LANES)
        lower = slice(column * LANES, (column + 1) * LANES)
        screen_ref[upper, lower] = tile
        screen_ref[lower, upper] = tile.T
    down = lax.broadcasted_iota(jnp.int32, (LANES, LANES), 0)
    across = lax.broadcasted_iota(jnp.int32, (LANES, LANES), 1)
    lines = packed_ref[packed_rows(aux_count)[0] :, :].astype(F32)
    for pair in range(aux_count // LANES // 2):
        n = len(places) + pair
        tile = packed_ref[n * LANES : (n + 1) * LANES, :].astype(F32)
        turned = tile.T
        first = slice(2 * pair * LANES, (2 * pair + 1) * LANES)
        second = slice((2 * pair + 1) * LANES, (2 * pair + 2) * LANES)
        screen_ref[first, first] = jnp.where(across >= down, tile, turned).astype(BF16)
        strict = jnp.where(across < down, tile, turned)
        screen_ref[second, second] = jnp.where(
            across == down, lines[pair : pair + 1], strict
        ).astype(BF16)
    screened_ref[...] = jnp.dot(
        coeffs_ref[...], screen_ref[...], preferred_element_type=F32
    ).astype(BF16)


def respond_half(screened_ref, held_ref, field_ref, inputs, outs, half, arrived=None):
    occ_ref, own_ref, other_ref = inputs
    term_ref, own_update_ref, other_update_ref = outs
    local_k, occ_count, _ = occ_ref.shape
    group_count = own_ref.shape[1]
    rows = occ_count * group_count
    span = term_ref.shape[2]
    width = held_ref.shape[2]

    def grid_of(step):
        return pl.ds(pl.multiple_of(half * span + step * width, width), width)

    def chunk(step, carry):
        to = pl.ds(pl.multiple_of(step * width, width), width)
        grid = grid_of(step)
        if arrived is not None:
            arrived(step)
        field_ref[...] = jnp.dot(
            screened_ref[...], held_ref[step], preferred_element_type=F32
        ).astype(BF16)
        for k in range(local_k):
            occ = occ_ref[k, :, grid].astype(F32)
            sums = [None] * occ_count
            sides = ((own_ref, own_update_ref), (other_ref, other_update_ref))
            for side, (virt_ref, update_ref) in enumerate(sides):
                virt = virt_ref[k, :, grid].astype(F32)
                first = (side * local_k + k) * rows
                virt_term = None
                for i in range(occ_count):
                    here = slice(first + i * group_count, first + (i + 1) * group_count)
                    piece = field_ref[here, :].astype(F32)
                    line = jnp.sum((piece * virt).reshape(group_count // 8, 8, width), axis=0)
                    sums[i] = line if side == 0 else sums[i] + line
                    product = piece * occ[i : i + 1]
                    virt_term = product if virt_term is None else virt_term + product
                update_ref[k, :, to] = virt_term.astype(BF16)
            term_ref[k, :, to] = jnp.concatenate(
                [jnp.sum(line, axis=0, keepdims=True) for line in sums], axis=0
            ).astype(BF16)
        return carry

    lax.fori_loop(0, span // width, chunk, 0)


def upper_half():
    return (lax.axis_index("band") // 2) % 2


def respond_far_kernel(
    coeffs_ref, packed_ref, occ_ref, own_ref, other_ref, basis_ref,
    term_ref, own_update_ref, other_update_ref, screened_ref, near_ref,
    screen_ref, far_ref, field_ref, far_sems, near_sem,
):
    steps, _, width = far_ref.shape
    far, near = 1 - upper_half(), upper_half()

    def fetch(half, step, held_ref, sem):
        start = pl.multiple_of((half * steps + step) * width, width)
        return pltpu.make_async_copy(
            basis_ref.at[:, pl.ds(start, width)], held_ref.at[step], sem
        )

    for step in range(steps):
        fetch(far, step, far_ref, far_sems.at[step]).start()
    for step in range(steps):
        fetch(near, step, near_ref, near_sem.at[step]).start()
    screen_coeffs(coeffs_ref, packed_ref, screen_ref, screened_ref)
    respond_half(
        screened_ref, far_ref, field_ref, (occ_ref, own_ref, other_ref),
        (term_ref, own_update_ref, other_update_ref), far,
        lambda step: fetch(far, step, far_ref, far_sems.at[step]).wait(),
    )
    for step in range(steps):
        fetch(near, step, near_ref, near_sem.at[step]).wait()


def respond_near_kernel(
    screened_ref, occ_ref, own_ref, other_ref, near_ref,
    term_ref, own_update_ref, other_update_ref, field_ref,
):
    respond_half(
        screened_ref, near_ref, field_ref, (occ_ref, own_ref, other_ref),
        (term_ref, own_update_ref, other_update_ref), upper_half(),
    )


def respond(coeffs, packed, basis, occ, own, other):
    local_k, occ_count, grid_count = occ.shape
    group_count = own.shape[1]
    rows, aux_count = coeffs.shape
    half = grid_count // 2
    width = min(1024, half)
    any_spec = pl.BlockSpec(memory_space=pl.ANY)
    shapes = [
        jax.ShapeDtypeStruct((local_k, occ_count, half), BF16),
        jax.ShapeDtypeStruct((local_k, group_count, half), BF16),
        jax.ShapeDtypeStruct((local_k, group_count, half), BF16),
    ]
    held = (half // width, aux_count, width)
    cost = pl.CostEstimate(
        flops=rows * grid_count * aux_count, bytes_accessed=4 << 20, transcendentals=0
    )
    *far, screened, near_basis = pl.pallas_call(
        respond_far_kernel,
        in_specs=[VMEM_SPEC] * 5 + [any_spec],
        out_specs=[VMEM_SPEC] * 5,
        out_shape=shapes
        + [jax.ShapeDtypeStruct(coeffs.shape, BF16), jax.ShapeDtypeStruct(held, BF16)],
        scratch_shapes=[
            pltpu.VMEM((aux_count, aux_count), BF16),
            pltpu.VMEM(held, BF16),
            pltpu.VMEM((rows, width), BF16),
            pltpu.SemaphoreType.DMA((held[0],)),
            pltpu.SemaphoreType.DMA((held[0],)),
        ],
        compiler_params=pltpu.CompilerParams(vmem_limit_bytes=FAR_VMEM),
        cost_estimate=cost,
        name="respond_far",
    )(coeffs, packed, occ, own, other, basis)
    near = pl.pallas_call(
        respond_near_kernel,
        in_specs=[VMEM_SPEC] * 5,
        out_specs=[VMEM_SPEC] * 3,
        out_shape=shapes,
        scratch_shapes=[pltpu.VMEM((rows, width), BF16)],
        compiler_params=pltpu.CompilerParams(vmem_limit_bytes=NEAR_VMEM),
        cost_estimate=cost,
        name="respond_near",
    )(screened, occ, own, other, near_basis)
    return far, near


def shards(occupied, virtual, occ_energy, virt_energy, partner, coulomb, basis):
    local_k, occ_count, grid_count = occupied.shape
    group_count = virtual.shape[1]
    aux_count = basis.shape[0]
    transfers = partner.shape[0]
    assert transfers == 2
    cube = Hypercube()
    total_k = local_k * cube.ka
    virt_count = group_count * cube.band
    gram_scale = 1.0 / math.sqrt(total_k * occ_count * virt_count * aux_count)
    occ_scale = 1.0 / math.sqrt(transfers * virt_count)
    ka = lax.axis_index("ka")

    first = cube.bit(cube.core) == 0
    other_virtual = cube.swap(virtual, cube.core)

    def level_rows(energy):
        rows = lax.dynamic_slice_in_dim(energy, ka * local_k, local_k, axis=0)
        return jnp.broadcast_to(rows[:, :, None], rows.shape + (LANES,))

    levels = jnp.concatenate(
        [level_rows(virt_energy), level_rows(cube.swap(virt_energy, cube.core))]
    )
    sources = partners_of(partner, ka, local_k)
    neighbour_sources = partners_of(partner, jnp.bitwise_xor(ka, 1), local_k)
    partner_occ, partner_energy, first_basis = fetch_partners(
        cube, occupied, occ_energy, sources, neighbour_sources, basis[:, : grid_count // 8]
    )
    partner_energy = jnp.broadcast_to(
        partner_energy[:, :, None], partner_energy.shape + (LANES,)
    )
    factors = jnp.where(first, coulomb[:1], coulomb[1:])
    coeffs, packed = project(
        partner_occ, virtual, other_virtual, first_basis, basis, partner_energy, levels, factors,
        gram_scale,
    )
    packed = reduce_screen(cube, packed)
    far, near = respond(coeffs, packed, basis, partner_occ, virtual, other_virtual)
    arrived = cube.swap(far[0], cube.y)
    terms = (near[0].astype(F32) + arrived.astype(F32)).astype(BF16)
    updates = [
        (own.astype(F32) + cube.swap(other, cube.core).astype(F32)).astype(BF16)
        for _, own, other in (far, near)
    ]
    lower = cube.bit(cube.y) == 0
    virt_update = jnp.concatenate(
        [jnp.where(lower, updates[1], updates[0]), jnp.where(lower, updates[0], updates[1])],
        axis=2,
    )
    occ_total, virt_update = return_occupied(
        cube, terms, local_k, sources, neighbour_sources, virt_update
    )
    return ((occ_total * occ_scale).astype(BF16), virt_update)


def solution(mesh):
    in_specs = (
        P("ka", None, None),
        P("ka", "band", None),
        P("ka", None),
        P(None, "band"),
        P(),
        P(),
        P(),
    )
    out_specs = (P("ka", None, "band"), P("ka", "band", None))
    return jax.shard_map(shards, mesh=mesh, in_specs=in_specs, out_specs=out_specs, check_vma=False)
```

```python
import functools
import math

import jax
import jax.numpy as jnp
from jax import lax
from jax.experimental import pallas as pl
from jax.experimental.pallas import tpu as pltpu
from jax.sharding import PartitionSpec as P

FREQUENCY = 2.5
BROADENING = 0.4
LANES = 128
PROJECT_VMEM = 48 << 20
FAR_VMEM = 45 << 20
NEAR_VMEM = 32 << 20
VMEM_SPEC = pl.BlockSpec(memory_space=pltpu.VMEM)
BF16 = jnp.bfloat16
F32 = jnp.float32


def response(energy_gaps):
    shifted = FREQUENCY - energy_gaps
    return shifted / (shifted * shifted + BROADENING * BROADENING)


def pick(stack, index):
    return lax.dynamic_index_in_dim(stack, index, 0, keepdims=False)


class Hypercube:
    def __init__(self):
        self.ka = lax.axis_size("ka")
        self.band = lax.axis_size("band")
        self.count = self.ka * self.band
        assert self.band == 4 and self.ka >= 2 and self.ka & (self.ka - 1) == 0
        self.index = lax.axis_index("ka") * self.band + lax.axis_index("band")
        self.core, self.y, self.x = 1, 2, 4
        rest = [bit for bit in (1 << n for n in range(3, 31)) if bit < self.count]
        self.groups = [rest[n : n + 2] for n in range(0, len(rest), 2)]

    def bit(self, mask):
        return (self.index // mask) % 2

    def swap(self, value, mask):
        return lax.ppermute(
            value, ("ka", "band"), [(device, device ^ mask) for device in range(self.count)]
        )


def masks_of(bits):
    return [sum(bit for n, bit in enumerate(bits) if (d >> n) & 1) for d in range(1, 1 << len(bits))]


def sum_scatter(cube, parts, bits):
    me = sum(cube.bit(bit) << n for n, bit in enumerate(bits))
    total = pick(parts, me).astype(F32)
    arrived = [
        cube.swap(pick(parts, jnp.bitwise_xor(me, d + 1)), mask)
        for d, mask in enumerate(masks_of(bits))
    ]
    for term in arrived:
        total = total + term.astype(F32)
    return total


def gather_differences(cube, value, bits):
    return jnp.stack([value] + [cube.swap(value, mask) for mask in masks_of(bits)])


def gather_parts(cube, value, bits):
    me = sum(cube.bit(bit) << n for n, bit in enumerate(bits))
    differences = gather_differences(cube, value, bits)
    return jnp.stack(
        [pick(differences, jnp.bitwise_xor(me, d)) for d in range(1 << len(bits))]
    )


def blocks_of(aux_count):
    count = aux_count // LANES
    return [(row, column) for row in range(count) for column in range(row + 1, count)]


def packed_rows(aux_count):
    count = aux_count // LANES
    assert count % 2 == 0
    blocks = (len(blocks_of(aux_count)) + count // 2) * LANES
    return blocks, blocks + 64


def split_float(value):
    high = lax.reduce_precision(value, 8, 7)
    middle = lax.reduce_precision(value - high, 8, 7)
    low = value - high - middle
    return high.astype(BF16), middle.astype(BF16), low.astype(BF16)


def partners_of(partner, device, local_k):
    every_k = jnp.arange(partner.shape[1], dtype=jnp.int32)
    own_k = device * local_k + jnp.arange(local_k, dtype=jnp.int32)
    here = every_k[None, None, :] == own_k[None, :, None]
    return jnp.sum(jnp.where(here, partner[:, None, :], 0), axis=2).reshape(-1)


def own_transfer_first(cube, values, local_k):
    first = cube.bit(cube.core) == 0
    low, high = values[:local_k], values[local_k:]
    return jnp.where(first, low, high), jnp.where(first, high, low)


def fetch_partners(cube, occupied, occ_energy, sources, neighbour_sources, make_beside):
    local_k, occ_count, grid_count = occupied.shape
    width = grid_count // cube.band
    ka = lax.axis_index("ka")
    first = cube.bit(cube.core) == 0
    quarter = lax.dynamic_slice_in_dim(occupied, lax.axis_index("band") * width, width, axis=2)
    pieces = jnp.stack(split_float(occ_energy), axis=2)
    payload = jnp.concatenate(
        [quarter, jnp.pad(pieces, ((0, 0), (0, 0), (0, LANES - pieces.shape[2])))], axis=2
    )
    gathered = payload[None]
    for bits in cube.groups:
        gathered = gather_differences(cube, gathered, bits).reshape((-1,) + payload.shape)
    gathered = gathered.reshape((-1,) + payload.shape[1:])
    gathered, late_ka, late_band = lax.optimization_barrier((gathered, ka, lax.axis_index("band")))
    beside = make_beside(late_ka, late_band)
    side, upper = ka % 2, ka // 2
    slots = jnp.arange(gathered.shape[0], dtype=jnp.int32)
    held = (jnp.bitwise_xor(slots // local_k, upper) * 2 + side) * local_k + slots % local_k

    def held_of(wanted):
        hits = wanted[:, None] == held[None, :]
        return jnp.sum(
            jnp.where(hits[:, :, None, None], gathered[None].astype(F32), 0.0), axis=1
        ).astype(BF16)

    own_sources, other_sources = own_transfer_first(cube, sources, local_k)
    own_neighbour, other_neighbour = own_transfer_first(cube, neighbour_sources, local_k)
    along_x = cube.swap(held_of(own_neighbour), cube.x)
    across = cube.swap(held_of(other_neighbour)[:, :, :width], cube.x | cube.core)
    beside_core = cube.swap(held_of(other_sources)[:, :, :width], cube.core)
    along_x, beside = lax.optimization_barrier((along_x, beside))
    mine = held_of(own_sources) + along_x
    other = beside_core + across
    energy = mine[:, :, width : width + 3].astype(F32)
    energy = (energy[:, :, 0] + energy[:, :, 1]) + energy[:, :, 2]
    part = mine[:, :, :width]
    part = jnp.concatenate([jnp.where(first, part, other), jnp.where(first, other, part)], axis=2)
    return part, cube.swap(part, cube.y), energy, beside


def reduce_screen(cube, own):
    rows = own.shape[0]
    piece = sum_scatter(cube, own.reshape(4, rows // 4, LANES), [cube.y, cube.x]).astype(BF16)
    for bits in cube.groups:
        arrived = [cube.swap(piece, mask) for mask in masks_of(bits)]
        total = piece.astype(F32)
        for term in arrived:
            total = total + term.astype(F32)
        piece = total.astype(BF16)
    return gather_parts(cube, piece, [cube.y, cube.x]).reshape(own.shape)


def return_occupied(cube, part, local_k, sources, neighbour_sources, beside):
    ka = lax.axis_index("ka")
    width = part.shape[2] // 2
    first = cube.bit(cube.core) == 0
    keep = jnp.where(first, part[:, :, :width], part[:, :, width:])
    give = jnp.where(first, part[:, :, width:], part[:, :, :width])
    along_x = cube.swap(keep, cube.x)
    across = cube.swap(give, cube.x | cube.core)
    beside_core = cube.swap(give, cube.core)
    side, upper = ka % 2, ka // 2
    both = jnp.concatenate([keep, beside_core, along_x, across], axis=0)
    targets = jnp.concatenate(
        own_transfer_first(cube, sources, local_k)
        + own_transfer_first(cube, neighbour_sources, local_k)
    )

    def placed(uppers):
        wanted_k = ((uppers * 2 + side) * local_k)[:, None] + jnp.arange(local_k, dtype=jnp.int32)
        hits = targets[None, None, :] == wanted_k[:, :, None]
        return jnp.sum(
            jnp.where(hits[:, :, :, None, None], both[None, None].astype(F32), 0.0), axis=2
        )

    spans = 1
    for bits in cube.groups:
        spans *= 1 << len(bits)
    differences = jnp.arange(spans, dtype=jnp.int32)
    value = placed(jnp.bitwise_xor(differences, upper))
    for bits in reversed(cube.groups):
        size = 1 << len(bits)
        value = value.reshape((size, -1) + value.shape[1:])
        total = value[0]
        arrived = [
            cube.swap(value[d + 1].astype(BF16), mask) for d, mask in enumerate(masks_of(bits))
        ]
        arrived[-1], beside = lax.optimization_barrier((arrived[-1], beside))
        for term in arrived:
            total = total + term.astype(F32)
        value = total
    return value[0], beside


def grid_copies(basis_ref, held_ref, sems, starts):
    ends = starts[1:] + [basis_ref.shape[1]]
    return [
        pltpu.make_async_copy(
            basis_ref.at[:, start:end], held_ref.at[:, start:end], sems.at[n]
        )
        for n, (start, end) in enumerate(zip(starts, ends))
    ]


def pair_coeffs(occ, virt, basis):
    pair_rows = jnp.concatenate([occ[i : i + 1] * virt for i in range(occ.shape[0])], axis=0)
    return lax.dot_general(
        pair_rows, basis, (((1,), (1,)), ((), ())), preferred_element_type=F32
    )


def upper_half():
    return (lax.axis_index("band") // 2) % 2


def project_near_kernel(
    occ_ref, own_ref, other_ref, first_ref, basis_ref, total_ref, far_ref, held_ref, sems, *, starts
):
    local_k, occ_count, half = occ_ref.shape
    rows = occ_count * own_ref.shape[1]
    near = pl.multiple_of(upper_half() * half, half)
    far = pl.multiple_of((1 - upper_half()) * half, half)
    parts = list(zip(starts, starts[1:] + (half,)))
    offset = starts[1]
    copies = [
        pltpu.make_async_copy(
            basis_ref.at[:, pl.ds(near + start, end - start)],
            held_ref.at[:, start - offset : end - offset],
            sems.at[n],
        )
        for n, (start, end) in enumerate(parts[1:])
    ]
    copies.append(
        pltpu.make_async_copy(basis_ref.at[:, pl.ds(far, half)], far_ref, sems.at[len(copies)])
    )
    for copy in copies:
        copy.start()
    terms = [(virt_ref, k) for virt_ref in (own_ref, other_ref) for k in range(local_k)]
    for n, (start, end) in enumerate(parts):
        if n > 0:
            copies[n - 1].wait()
        for term, (virt_ref, k) in enumerate(terms):
            part = pair_coeffs(
                occ_ref[k, :, start:end],
                virt_ref[k, :, pl.ds(near + start, end - start)],
                held_ref[:, start - offset : end - offset] if n > 0 else first_ref[...],
            )
            here = slice(term * rows, (term + 1) * rows)
            total_ref[here, :] = total_ref[here, :] + part if n > 0 else part
    copies[-1].wait()


def project_kernel(
    occ_ref, own_ref, other_ref, occ_energy_ref, levels_ref, coulomb_ref, total_ref, basis_ref,
    coeffs_ref, gram_ref, weighted_ref, *, scale,
):
    local_k, occ_count, half = occ_ref.shape
    group_count = own_ref.shape[1]
    aux_count = basis_ref.shape[0]
    rows = occ_count * group_count
    count = aux_count // LANES
    far = pl.multiple_of((1 - upper_half()) * half, half)
    terms = [(virt_ref, k) for virt_ref in (own_ref, other_ref) for k in range(local_k)]
    for term, (virt_ref, k) in enumerate(terms):
        here = slice(term * rows, (term + 1) * rows)
        part = pair_coeffs(occ_ref[k], virt_ref[k, :, pl.ds(far, half)], basis_ref[...])
        coeffs = (total_ref[here, :] + part).astype(BF16)
        coeffs_ref[here, :] = coeffs
        for i in range(occ_count):
            first = i * group_count
            weights = response(levels_ref[term] - occ_energy_ref[k][i : i + 1])
            values = coeffs[first : first + group_count].astype(F32)
            weighted_ref[term * rows + first : term * rows + first + group_count, :] = (
                jnp.concatenate(
                    [values[:, n * LANES : (n + 1) * LANES] * weights for n in range(count)],
                    axis=1,
                ).astype(BF16)
            )
    coulomb = coulomb_ref[...] * math.sqrt(scale)
    tiles = {}
    for panel in range(0, count, 2):
        gram = lax.dot_general(
            weighted_ref[:, panel * LANES : (panel + 2) * LANES],
            coeffs_ref[:, panel * LANES :],
            (((0,), (0,)), ((), ())),
            preferred_element_type=F32,
        )
        for row in (panel, panel + 1):
            left = jnp.broadcast_to(coulomb[:, row * LANES : (row + 1) * LANES], (LANES, LANES)).T
            for column in range(row, count):
                down, across = (row - panel) * LANES, (column - panel) * LANES
                right = coulomb[:, column * LANES : (column + 1) * LANES]
                tiles[row, column] = (
                    left * gram[down : down + LANES, across : across + LANES] * right
                )
    places = blocks_of(aux_count)
    for n, place in enumerate(places):
        gram_ref[n * LANES : (n + 1) * LANES, :] = tiles[place].astype(BF16)
    down = lax.broadcasted_iota(jnp.int32, (LANES, LANES), 0)
    across = lax.broadcasted_iota(jnp.int32, (LANES, LANES), 1)
    lines = []
    for pair in range(count // 2):
        upper, lower = tiles[2 * pair, 2 * pair], tiles[2 * pair + 1, 2 * pair + 1]
        n = len(places) + pair
        gram_ref[n * LANES : (n + 1) * LANES, :] = jnp.where(across >= down, upper, lower).astype(
            BF16
        )
        lines.append(jnp.sum(jnp.where(across == down, lower, 0.0), axis=0, keepdims=True))
    blocks, total_rows = packed_rows(aux_count)
    lines.append(jnp.zeros((total_rows - blocks - len(lines), LANES), F32))
    gram_ref[blocks:, :] = jnp.concatenate(lines, axis=0).astype(BF16)


def project(near_occ, far_occ, own, other, first, basis, occ_energy, levels, coulomb, scale):
    local_k, occ_count, half = near_occ.shape
    group_count = own.shape[1]
    aux_count = basis.shape[0]
    rows = 2 * local_k * occ_count * group_count
    width = first.shape[1]
    starts = (0, width, 2 * width)
    cost = pl.CostEstimate(
        flops=2 * rows * half * aux_count, bytes_accessed=4 << 20, transcendentals=0
    )
    total, far_basis = pl.pallas_call(
        functools.partial(project_near_kernel, starts=starts),
        in_specs=[VMEM_SPEC] * 4 + [pl.BlockSpec(memory_space=pl.ANY)],
        out_specs=[VMEM_SPEC] * 2,
        out_shape=[
            jax.ShapeDtypeStruct((rows, aux_count), F32),
            jax.ShapeDtypeStruct((aux_count, half), BF16),
        ],
        scratch_shapes=[
            pltpu.VMEM((aux_count, half - width), BF16),
            pltpu.SemaphoreType.DMA((len(starts),)),
        ],
        compiler_params=pltpu.CompilerParams(vmem_limit_bytes=PROJECT_VMEM),
        cost_estimate=cost,
        name="project_near",
    )(near_occ, own, other, first, basis)
    return pl.pallas_call(
        functools.partial(project_kernel, scale=scale),
        in_specs=[VMEM_SPEC] * 8,
        out_specs=[VMEM_SPEC] * 2,
        out_shape=[
            jax.ShapeDtypeStruct((rows, aux_count), BF16),
            jax.ShapeDtypeStruct((packed_rows(aux_count)[1], LANES), BF16),
        ],
        scratch_shapes=[pltpu.VMEM((rows, aux_count), BF16)],
        compiler_params=pltpu.CompilerParams(vmem_limit_bytes=NEAR_VMEM),
        cost_estimate=cost,
        name="project",
    )(far_occ, own, other, occ_energy, levels, coulomb, total, far_basis)


def screen_coeffs(coeffs_ref, packed_ref, screen_ref, screened_ref):
    aux_count = coeffs_ref.shape[1]
    places = blocks_of(aux_count)
    for n, (row, column) in enumerate(places):
        tile = packed_ref[n * LANES : (n + 1) * LANES, :]
        upper = slice(row * LANES, (row + 1) * LANES)
        lower = slice(column * LANES, (column + 1) * LANES)
        screen_ref[upper, lower] = tile
        screen_ref[lower, upper] = tile.T
    down = lax.broadcasted_iota(jnp.int32, (LANES, LANES), 0)
    across = lax.broadcasted_iota(jnp.int32, (LANES, LANES), 1)
    lines = packed_ref[packed_rows(aux_count)[0] :, :].astype(F32)
    for pair in range(aux_count // LANES // 2):
        n = len(places) + pair
        tile = packed_ref[n * LANES : (n + 1) * LANES, :].astype(F32)
        turned = tile.T
        first = slice(2 * pair * LANES, (2 * pair + 1) * LANES)
        second = slice((2 * pair + 1) * LANES, (2 * pair + 2) * LANES)
        screen_ref[first, first] = jnp.where(across >= down, tile, turned).astype(BF16)
        strict = jnp.where(across < down, tile, turned)
        screen_ref[second, second] = jnp.where(
            across == down, lines[pair : pair + 1], strict
        ).astype(BF16)
    screened_ref[...] = jnp.dot(
        coeffs_ref[...], screen_ref[...], preferred_element_type=F32
    ).astype(BF16)


def respond_half(screened_ref, held_ref, field_ref, inputs, outs, half, arrived=None):
    occ_ref, own_ref, other_ref = inputs
    term_ref, own_update_ref, other_update_ref = outs
    local_k, occ_count, _ = occ_ref.shape
    group_count = own_ref.shape[1]
    rows = occ_count * group_count
    span = term_ref.shape[2]
    width = held_ref.shape[2]

    def grid_of(step):
        return pl.ds(pl.multiple_of(half * span + step * width, width), width)

    def chunk(step, carry):
        to = pl.ds(pl.multiple_of(step * width, width), width)
        grid = grid_of(step)
        if arrived is not None:
            arrived(step)
        field_ref[...] = jnp.dot(
            screened_ref[...], held_ref[step], preferred_element_type=F32
        ).astype(BF16)
        for k in range(local_k):
            occ = occ_ref[k, :, to].astype(F32)
            sums = [None] * occ_count
            sides = ((own_ref, own_update_ref), (other_ref, other_update_ref))
            for side, (virt_ref, update_ref) in enumerate(sides):
                virt = virt_ref[k, :, grid].astype(F32)
                first = (side * local_k + k) * rows
                virt_term = None
                for i in range(occ_count):
                    here = slice(first + i * group_count, first + (i + 1) * group_count)
                    piece = field_ref[here, :].astype(F32)
                    line = jnp.sum((piece * virt).reshape(group_count // 8, 8, width), axis=0)
                    sums[i] = line if side == 0 else sums[i] + line
                    product = piece * occ[i : i + 1]
                    virt_term = product if virt_term is None else virt_term + product
                update_ref[k, :, to] = virt_term.astype(BF16)
            term_ref[k, :, to] = jnp.concatenate(
                [jnp.sum(line, axis=0, keepdims=True) for line in sums], axis=0
            ).astype(BF16)
        return carry

    lax.fori_loop(0, span // width, chunk, 0)


def respond_far_kernel(
    coeffs_ref, packed_ref, occ_ref, own_ref, other_ref, basis_ref,
    term_ref, own_update_ref, other_update_ref, screened_ref, near_ref,
    screen_ref, far_ref, field_ref, far_sems, near_sem,
):
    steps, _, width = far_ref.shape
    far, near = 1 - upper_half(), upper_half()

    def fetch(half, step, held_ref, sem):
        start = pl.multiple_of((half * steps + step) * width, width)
        return pltpu.make_async_copy(
            basis_ref.at[:, pl.ds(start, width)], held_ref.at[step], sem
        )

    for step in range(steps):
        fetch(far, step, far_ref, far_sems.at[step]).start()
    for step in range(steps):
        fetch(near, step, near_ref, near_sem.at[step]).start()
    screen_coeffs(coeffs_ref, packed_ref, screen_ref, screened_ref)
    respond_half(
        screened_ref, far_ref, field_ref, (occ_ref, own_ref, other_ref),
        (term_ref, own_update_ref, other_update_ref), far,
        lambda step: fetch(far, step, far_ref, far_sems.at[step]).wait(),
    )
    for step in range(steps):
        fetch(near, step, near_ref, near_sem.at[step]).wait()


def respond_near_kernel(
    screened_ref, occ_ref, own_ref, other_ref, near_ref,
    term_ref, own_update_ref, other_update_ref, field_ref,
):
    respond_half(
        screened_ref, near_ref, field_ref, (occ_ref, own_ref, other_ref),
        (term_ref, own_update_ref, other_update_ref), upper_half(),
    )


def respond(coeffs, packed, basis, near_occ, far_occ, own, other):
    local_k, occ_count, half = near_occ.shape
    grid_count = 2 * half
    group_count = own.shape[1]
    rows, aux_count = coeffs.shape
    width = min(1024, half)
    any_spec = pl.BlockSpec(memory_space=pl.ANY)
    shapes = [
        jax.ShapeDtypeStruct((local_k, occ_count, half), BF16),
        jax.ShapeDtypeStruct((local_k, group_count, half), BF16),
        jax.ShapeDtypeStruct((local_k, group_count, half), BF16),
    ]
    held = (half // width, aux_count, width)
    cost = pl.CostEstimate(
        flops=rows * grid_count * aux_count, bytes_accessed=4 << 20, transcendentals=0
    )
    *far, screened, near_basis = pl.pallas_call(
        respond_far_kernel,
        in_specs=[VMEM_SPEC] * 5 + [any_spec],
        out_specs=[VMEM_SPEC] * 5,
        out_shape=shapes
        + [jax.ShapeDtypeStruct(coeffs.shape, BF16), jax.ShapeDtypeStruct(held, BF16)],
        scratch_shapes=[
            pltpu.VMEM((aux_count, aux_count), BF16),
            pltpu.VMEM(held, BF16),
            pltpu.VMEM((rows, width), BF16),
            pltpu.SemaphoreType.DMA((held[0],)),
            pltpu.SemaphoreType.DMA((held[0],)),
        ],
        compiler_params=pltpu.CompilerParams(vmem_limit_bytes=FAR_VMEM),
        cost_estimate=cost,
        name="respond_far",
    )(coeffs, packed, far_occ, own, other, basis)
    near = pl.pallas_call(
        respond_near_kernel,
        in_specs=[VMEM_SPEC] * 5,
        out_specs=[VMEM_SPEC] * 3,
        out_shape=shapes,
        scratch_shapes=[pltpu.VMEM((rows, width), BF16)],
        compiler_params=pltpu.CompilerParams(vmem_limit_bytes=NEAR_VMEM),
        cost_estimate=cost,
        name="respond_near",
    )(screened, near_occ, own, other, near_basis)
    return far, near


def shards(occupied, virtual, occ_energy, virt_energy, partner, coulomb, basis):
    local_k, occ_count, grid_count = occupied.shape
    group_count = virtual.shape[1]
    aux_count = basis.shape[0]
    transfers = partner.shape[0]
    assert transfers == 2
    cube = Hypercube()
    total_k = local_k * cube.ka
    virt_count = group_count * cube.band
    gram_scale = 1.0 / math.sqrt(total_k * occ_count * virt_count * aux_count)
    occ_scale = 1.0 / math.sqrt(transfers * virt_count)
    ka = lax.axis_index("ka")

    other_virtual = cube.swap(virtual, cube.core)
    other_energy = cube.swap(virt_energy, cube.core)

    def operands(late_ka, late_band):
        def level_rows(energy):
            rows = lax.dynamic_slice_in_dim(energy, late_ka * local_k, local_k, axis=0)
            return jnp.broadcast_to(rows[:, :, None], rows.shape + (LANES,))

        levels = jnp.concatenate([level_rows(virt_energy), level_rows(other_energy)])
        near_start = (late_band // 2) % 2 * (grid_count // 2)
        first_basis = lax.dynamic_slice_in_dim(basis, near_start, grid_count // 8, axis=1)
        factors = jnp.where(late_band % 2 == 0, coulomb[:1], coulomb[1:])
        return levels, first_basis, factors

    sources = partners_of(partner, ka, local_k)
    neighbour_sources = partners_of(partner, jnp.bitwise_xor(ka, 1), local_k)
    near_occ, far_occ, partner_energy, (levels, first_basis, factors) = fetch_partners(
        cube, occupied, occ_energy, sources, neighbour_sources, operands
    )
    partner_energy = jnp.broadcast_to(
        partner_energy[:, :, None], partner_energy.shape + (LANES,)
    )
    coeffs, packed = project(
        near_occ, far_occ, virtual, other_virtual, first_basis, basis, partner_energy, levels, factors,
        gram_scale,
    )
    packed = reduce_screen(cube, packed)
    far, near = respond(coeffs, packed, basis, near_occ, far_occ, virtual, other_virtual)
    arrived = cube.swap(far[0], cube.y)
    terms = (near[0].astype(F32) + arrived.astype(F32)).astype(BF16)
    updates = [
        (own.astype(F32) + cube.swap(other, cube.core).astype(F32)).astype(BF16)
        for _, own, other in (far, near)
    ]
    lower = cube.bit(cube.y) == 0
    virt_update = jnp.concatenate(
        [jnp.where(lower, updates[1], updates[0]), jnp.where(lower, updates[0], updates[1])],
        axis=2,
    )
    occ_total, virt_update = return_occupied(
        cube, terms, local_k, sources, neighbour_sources, virt_update
    )
    return ((occ_total * occ_scale).astype(BF16), virt_update)


def solution(mesh):
    in_specs = (
        P("ka", None, None),
        P("ka", "band", None),
        P("ka", None),
        P(None, "band"),
        P(),
        P(),
        P(),
    )
    out_specs = (P("ka", None, "band"), P("ka", "band", None))
    return jax.shard_map(shards, mesh=mesh, in_specs=in_specs, out_specs=out_specs, check_vma=False)
```

```python
import functools
import math

import jax
import jax.numpy as jnp
from jax import lax
from jax.experimental import pallas as pl
from jax.experimental.pallas import tpu as pltpu
from jax.sharding import PartitionSpec as P

FREQUENCY = 2.5
BROADENING = 0.4
LANES = 128
PROJECT_VMEM = 48 << 20
FAR_VMEM = 45 << 20
NEAR_VMEM = 32 << 20
VMEM_SPEC = pl.BlockSpec(memory_space=pltpu.VMEM)
BF16 = jnp.bfloat16
F32 = jnp.float32


def response(energy_gaps):
    shifted = FREQUENCY - energy_gaps
    return shifted / (shifted * shifted + BROADENING * BROADENING)


def pick(stack, index):
    return lax.dynamic_index_in_dim(stack, index, 0, keepdims=False)


class Hypercube:
    def __init__(self):
        self.ka = lax.axis_size("ka")
        self.band = lax.axis_size("band")
        self.count = self.ka * self.band
        assert self.band == 4 and self.ka >= 2 and self.ka & (self.ka - 1) == 0
        self.index = lax.axis_index("ka") * self.band + lax.axis_index("band")
        self.core, self.y, self.x = 1, 2, 4
        rest = [bit for bit in (1 << n for n in range(3, 31)) if bit < self.count]
        self.groups = [rest[n : n + 2] for n in range(0, len(rest), 2)]

    def bit(self, mask):
        return (self.index // mask) % 2

    def swap(self, value, mask):
        return lax.ppermute(
            value, ("ka", "band"), [(device, device ^ mask) for device in range(self.count)]
        )


def masks_of(bits):
    return [sum(bit for n, bit in enumerate(bits) if (d >> n) & 1) for d in range(1, 1 << len(bits))]


def sum_scatter(cube, parts, bits):
    me = sum(cube.bit(bit) << n for n, bit in enumerate(bits))
    total = pick(parts, me).astype(F32)
    arrived = [
        cube.swap(pick(parts, jnp.bitwise_xor(me, d + 1)), mask)
        for d, mask in enumerate(masks_of(bits))
    ]
    for term in arrived:
        total = total + term.astype(F32)
    return total


def gather_differences(cube, value, bits):
    return jnp.stack([value] + [cube.swap(value, mask) for mask in masks_of(bits)])


def gather_parts(cube, value, bits):
    me = sum(cube.bit(bit) << n for n, bit in enumerate(bits))
    differences = gather_differences(cube, value, bits)
    return jnp.stack(
        [pick(differences, jnp.bitwise_xor(me, d)) for d in range(1 << len(bits))]
    )


def blocks_of(aux_count):
    count = aux_count // LANES
    return [(row, column) for row in range(count) for column in range(row + 1, count)]


def packed_rows(aux_count):
    count = aux_count // LANES
    assert count % 2 == 0
    blocks = (len(blocks_of(aux_count)) + count // 2) * LANES
    return blocks, blocks + 64


def split_float(value):
    high = lax.reduce_precision(value, 8, 7)
    middle = lax.reduce_precision(value - high, 8, 7)
    low = value - high - middle
    return high.astype(BF16), middle.astype(BF16), low.astype(BF16)


def partners_of(partner, device, local_k):
    every_k = jnp.arange(partner.shape[1], dtype=jnp.int32)
    own_k = device * local_k + jnp.arange(local_k, dtype=jnp.int32)
    here = every_k[None, None, :] == own_k[None, :, None]
    return jnp.sum(jnp.where(here, partner[:, None, :], 0), axis=2).reshape(-1)


def own_transfer_first(cube, values, local_k):
    first = cube.bit(cube.core) == 0
    low, high = values[:local_k], values[local_k:]
    return jnp.where(first, low, high), jnp.where(first, high, low)


def fetch_partners(cube, occupied, occ_energy, sources, neighbour_sources, make_beside):
    local_k, occ_count, grid_count = occupied.shape
    width = grid_count // cube.band
    ka = lax.axis_index("ka")
    first = cube.bit(cube.core) == 0
    quarter = lax.dynamic_slice_in_dim(occupied, lax.axis_index("band") * width, width, axis=2)
    pieces = jnp.stack(split_float(occ_energy), axis=2)
    payload = jnp.concatenate(
        [quarter, jnp.pad(pieces, ((0, 0), (0, 0), (0, LANES - pieces.shape[2])))], axis=2
    )
    gathered = payload[None]
    for bits in cube.groups:
        gathered = gather_differences(cube, gathered, bits).reshape((-1,) + payload.shape)
    gathered = gathered.reshape((-1,) + payload.shape[1:])
    gathered, late_ka, late_band = lax.optimization_barrier((gathered, ka, lax.axis_index("band")))
    beside = make_beside(late_ka, late_band)
    side, upper = ka % 2, ka // 2
    slots = jnp.arange(gathered.shape[0], dtype=jnp.int32)
    held = (jnp.bitwise_xor(slots // local_k, upper) * 2 + side) * local_k + slots % local_k

    def held_of(wanted):
        hits = wanted[:, None] == held[None, :]
        return jnp.sum(
            jnp.where(hits[:, :, None, None], gathered[None].astype(F32), 0.0), axis=1
        ).astype(BF16)

    own_sources, other_sources = own_transfer_first(cube, sources, local_k)
    own_neighbour, other_neighbour = own_transfer_first(cube, neighbour_sources, local_k)
    along_x = cube.swap(held_of(own_neighbour), cube.x)
    across = cube.swap(held_of(other_neighbour)[:, :, :width], cube.x | cube.core)
    beside_core = cube.swap(held_of(other_sources)[:, :, :width], cube.core)
    along_x, beside = lax.optimization_barrier((along_x, beside))
    mine = held_of(own_sources) + along_x
    other = beside_core + across
    energy = mine[:, :, width : width + 3].astype(F32)
    energy = (energy[:, :, 0] + energy[:, :, 1]) + energy[:, :, 2]
    part = mine[:, :, :width]
    part = jnp.concatenate([jnp.where(first, part, other), jnp.where(first, other, part)], axis=2)
    return part, cube.swap(part, cube.y), energy, beside


def reduce_screen(cube, own):
    rows = own.shape[0]
    piece = sum_scatter(cube, own.reshape(4, rows // 4, LANES), [cube.y, cube.x]).astype(BF16)
    for bits in cube.groups:
        arrived = [cube.swap(piece, mask) for mask in masks_of(bits)]
        total = piece.astype(F32)
        for term in arrived:
            total = total + term.astype(F32)
        piece = total.astype(BF16)
    return gather_parts(cube, piece, [cube.y, cube.x]).reshape(own.shape)


def return_occupied(cube, part, local_k, sources, neighbour_sources, beside):
    ka = lax.axis_index("ka")
    width = part.shape[2] // 2
    first = cube.bit(cube.core) == 0
    keep = jnp.where(first, part[:, :, :width], part[:, :, width:])
    give = jnp.where(first, part[:, :, width:], part[:, :, :width])
    along_x = cube.swap(keep, cube.x)
    across = cube.swap(give, cube.x | cube.core)
    beside_core = cube.swap(give, cube.core)
    side, upper = ka % 2, ka // 2
    both = jnp.concatenate([keep, beside_core, along_x, across], axis=0)
    targets = jnp.concatenate(
        own_transfer_first(cube, sources, local_k)
        + own_transfer_first(cube, neighbour_sources, local_k)
    )

    def placed(uppers):
        wanted_k = ((uppers * 2 + side) * local_k)[:, None] + jnp.arange(local_k, dtype=jnp.int32)
        hits = targets[None, None, :] == wanted_k[:, :, None]
        return jnp.sum(
            jnp.where(hits[:, :, :, None, None], both[None, None].astype(F32), 0.0), axis=2
        )

    spans = 1
    for bits in cube.groups:
        spans *= 1 << len(bits)
    differences = jnp.arange(spans, dtype=jnp.int32)
    value = placed(jnp.bitwise_xor(differences, upper))
    for bits in reversed(cube.groups):
        size = 1 << len(bits)
        value = value.reshape((size, -1) + value.shape[1:])
        total = value[0]
        arrived = [
            cube.swap(value[d + 1].astype(BF16), mask) for d, mask in enumerate(masks_of(bits))
        ]
        arrived[-1], beside = lax.optimization_barrier((arrived[-1], beside))
        for term in arrived:
            total = total + term.astype(F32)
        value = total
    return value[0], beside


def grid_copies(basis_ref, held_ref, sems, starts):
    ends = starts[1:] + [basis_ref.shape[1]]
    return [
        pltpu.make_async_copy(
            basis_ref.at[:, start:end], held_ref.at[:, start:end], sems.at[n]
        )
        for n, (start, end) in enumerate(zip(starts, ends))
    ]


def pair_coeffs(occ, virt, basis):
    pair_rows = jnp.concatenate([occ[i : i + 1] * virt for i in range(occ.shape[0])], axis=0)
    return lax.dot_general(
        pair_rows, basis, (((1,), (1,)), ((), ())), preferred_element_type=F32
    )


def upper_half():
    return (lax.axis_index("band") // 2) % 2


def project_near_kernel(
    occ_ref, own_ref, other_ref, first_ref, basis_ref, total_ref, far_ref, held_ref, sems, *, starts
):
    local_k, occ_count, half = occ_ref.shape
    rows = occ_count * own_ref.shape[1]
    near = pl.multiple_of(upper_half() * half, half)
    far = pl.multiple_of((1 - upper_half()) * half, half)
    parts = list(zip(starts, starts[1:] + (half,)))
    offset = starts[1]
    copies = [
        pltpu.make_async_copy(
            basis_ref.at[:, pl.ds(near + start, end - start)],
            held_ref.at[:, start - offset : end - offset],
            sems.at[n],
        )
        for n, (start, end) in enumerate(parts[1:])
    ]
    copies.append(
        pltpu.make_async_copy(basis_ref.at[:, pl.ds(far, half)], far_ref, sems.at[len(copies)])
    )
    for copy in copies[:-1]:
        copy.start()
    terms = [(virt_ref, k) for virt_ref in (own_ref, other_ref) for k in range(local_k)]
    for n, (start, end) in enumerate(parts):
        if n > 0:
            copies[n - 1].wait()
        if n == 1:
            copies[-1].start()
        for term, (virt_ref, k) in enumerate(terms):
            part = pair_coeffs(
                occ_ref[k, :, start:end],
                virt_ref[k, :, pl.ds(near + start, end - start)],
                held_ref[:, start - offset : end - offset] if n > 0 else first_ref[...],
            )
            here = slice(term * rows, (term + 1) * rows)
            total_ref[here, :] = total_ref[here, :] + part if n > 0 else part
    copies[-1].wait()


def project_kernel(
    occ_ref, own_ref, other_ref, occ_energy_ref, levels_ref, coulomb_ref, total_ref, basis_ref,
    coeffs_ref, gram_ref, weighted_ref, *, scale,
):
    local_k, occ_count, half = occ_ref.shape
    group_count = own_ref.shape[1]
    aux_count = basis_ref.shape[0]
    rows = occ_count * group_count
    count = aux_count // LANES
    far = pl.multiple_of((1 - upper_half()) * half, half)
    terms = [(virt_ref, k) for virt_ref in (own_ref, other_ref) for k in range(local_k)]
    for term, (virt_ref, k) in enumerate(terms):
        here = slice(term * rows, (term + 1) * rows)
        part = pair_coeffs(occ_ref[k], virt_ref[k, :, pl.ds(far, half)], basis_ref[...])
        coeffs = (total_ref[here, :] + part).astype(BF16)
        coeffs_ref[here, :] = coeffs
        for i in range(occ_count):
            first = i * group_count
            weights = response(levels_ref[term] - occ_energy_ref[k][i : i + 1])
            values = coeffs[first : first + group_count].astype(F32)
            weighted_ref[term * rows + first : term * rows + first + group_count, :] = (
                jnp.concatenate(
                    [values[:, n * LANES : (n + 1) * LANES] * weights for n in range(count)],
                    axis=1,
                ).astype(BF16)
            )
    own_transfer = lax.axis_index("band") % 2
    coulomb = coulomb_ref[pl.ds(own_transfer, 1), :] * math.sqrt(scale)
    tiles = {}
    for panel in range(0, count, 2):
        gram = lax.dot_general(
            weighted_ref[:, panel * LANES : (panel + 2) * LANES],
            coeffs_ref[:, panel * LANES :],
            (((0,), (0,)), ((), ())),
            preferred_element_type=F32,
        )
        for row in (panel, panel + 1):
            left = jnp.broadcast_to(coulomb[:, row * LANES : (row + 1) * LANES], (LANES, LANES)).T
            for column in range(row, count):
                down, across = (row - panel) * LANES, (column - panel) * LANES
                right = coulomb[:, column * LANES : (column + 1) * LANES]
                tiles[row, column] = (
                    left * gram[down : down + LANES, across : across + LANES] * right
                )
    places = blocks_of(aux_count)
    for n, place in enumerate(places):
        gram_ref[n * LANES : (n + 1) * LANES, :] = tiles[place].astype(BF16)
    down = lax.broadcasted_iota(jnp.int32, (LANES, LANES), 0)
    across = lax.broadcasted_iota(jnp.int32, (LANES, LANES), 1)
    lines = []
    for pair in range(count // 2):
        upper, lower = tiles[2 * pair, 2 * pair], tiles[2 * pair + 1, 2 * pair + 1]
        n = len(places) + pair
        gram_ref[n * LANES : (n + 1) * LANES, :] = jnp.where(across >= down, upper, lower).astype(
            BF16
        )
        lines.append(jnp.sum(jnp.where(across == down, lower, 0.0), axis=0, keepdims=True))
    blocks, total_rows = packed_rows(aux_count)
    lines.append(jnp.zeros((total_rows - blocks - len(lines), LANES), F32))
    gram_ref[blocks:, :] = jnp.concatenate(lines, axis=0).astype(BF16)


def project(near_occ, far_occ, own, other, first, basis, occ_energy, levels, coulomb, scale):
    local_k, occ_count, half = near_occ.shape
    group_count = own.shape[1]
    aux_count = basis.shape[0]
    rows = 2 * local_k * occ_count * group_count
    width = first.shape[1]
    starts = (0, width, 2 * width)
    cost = pl.CostEstimate(
        flops=2 * rows * half * aux_count, bytes_accessed=4 << 20, transcendentals=0
    )
    total, far_basis = pl.pallas_call(
        functools.partial(project_near_kernel, starts=starts),
        in_specs=[VMEM_SPEC] * 4 + [pl.BlockSpec(memory_space=pl.ANY)],
        out_specs=[VMEM_SPEC] * 2,
        out_shape=[
            jax.ShapeDtypeStruct((rows, aux_count), F32),
            jax.ShapeDtypeStruct((aux_count, half), BF16),
        ],
        scratch_shapes=[
            pltpu.VMEM((aux_count, half - width), BF16),
            pltpu.SemaphoreType.DMA((len(starts),)),
        ],
        compiler_params=pltpu.CompilerParams(vmem_limit_bytes=PROJECT_VMEM),
        cost_estimate=cost,
        name="project_near",
    )(near_occ, own, other, first, basis)
    return pl.pallas_call(
        functools.partial(project_kernel, scale=scale),
        in_specs=[VMEM_SPEC] * 8,
        out_specs=[VMEM_SPEC] * 2,
        out_shape=[
            jax.ShapeDtypeStruct((rows, aux_count), BF16),
            jax.ShapeDtypeStruct((packed_rows(aux_count)[1], LANES), BF16),
        ],
        scratch_shapes=[pltpu.VMEM((rows, aux_count), BF16)],
        compiler_params=pltpu.CompilerParams(vmem_limit_bytes=NEAR_VMEM),
        cost_estimate=cost,
        name="project",
    )(far_occ, own, other, occ_energy, levels, coulomb, total, far_basis)


def screen_coeffs(coeffs_ref, packed_ref, screen_ref, screened_ref):
    aux_count = coeffs_ref.shape[1]
    places = blocks_of(aux_count)
    for n, (row, column) in enumerate(places):
        tile = packed_ref[n * LANES : (n + 1) * LANES, :]
        upper = slice(row * LANES, (row + 1) * LANES)
        lower = slice(column * LANES, (column + 1) * LANES)
        screen_ref[upper, lower] = tile
        screen_ref[lower, upper] = tile.T
    down = lax.broadcasted_iota(jnp.int32, (LANES, LANES), 0)
    across = lax.broadcasted_iota(jnp.int32, (LANES, LANES), 1)
    lines = packed_ref[packed_rows(aux_count)[0] :, :].astype(F32)
    for pair in range(aux_count // LANES // 2):
        n = len(places) + pair
        tile = packed_ref[n * LANES : (n + 1) * LANES, :].astype(F32)
        turned = tile.T
        first = slice(2 * pair * LANES, (2 * pair + 1) * LANES)
        second = slice((2 * pair + 1) * LANES, (2 * pair + 2) * LANES)
        screen_ref[first, first] = jnp.where(across >= down, tile, turned).astype(BF16)
        strict = jnp.where(across < down, tile, turned)
        screen_ref[second, second] = jnp.where(
            across == down, lines[pair : pair + 1], strict
        ).astype(BF16)
    screened_ref[...] = jnp.dot(
        coeffs_ref[...], screen_ref[...], preferred_element_type=F32
    ).astype(BF16)


def respond_half(screened_ref, held_ref, field_ref, inputs, outs, half, arrived=None):
    occ_ref, own_ref, other_ref = inputs
    term_ref, own_update_ref, other_update_ref = outs
    local_k, occ_count, _ = occ_ref.shape
    group_count = own_ref.shape[1]
    rows = occ_count * group_count
    span = term_ref.shape[2]
    width = held_ref.shape[2]

    def grid_of(step):
        return pl.ds(pl.multiple_of(half * span + step * width, width), width)

    def chunk(step, carry):
        to = pl.ds(pl.multiple_of(step * width, width), width)
        grid = grid_of(step)
        if arrived is not None:
            arrived(step)
        field_ref[...] = jnp.dot(
            screened_ref[...], held_ref[step], preferred_element_type=F32
        ).astype(BF16)
        for k in range(local_k):
            occ = occ_ref[k, :, to].astype(F32)
            sums = [None] * occ_count
            sides = ((own_ref, own_update_ref), (other_ref, other_update_ref))
            for side, (virt_ref, update_ref) in enumerate(sides):
                virt = virt_ref[k, :, grid].astype(F32)
                first = (side * local_k + k) * rows
                virt_term = None
                for i in range(occ_count):
                    here = slice(first + i * group_count, first + (i + 1) * group_count)
                    piece = field_ref[here, :].astype(F32)
                    line = jnp.sum((piece * virt).reshape(group_count // 8, 8, width), axis=0)
                    sums[i] = line if side == 0 else sums[i] + line
                    product = piece * occ[i : i + 1]
                    virt_term = product if virt_term is None else virt_term + product
                update_ref[k, :, to] = virt_term.astype(BF16)
            term_ref[k, :, to] = jnp.concatenate(
                [jnp.sum(line, axis=0, keepdims=True) for line in sums], axis=0
            ).astype(BF16)
        return carry

    lax.fori_loop(0, span // width, chunk, 0)


def respond_far_kernel(
    coeffs_ref, packed_ref, occ_ref, own_ref, other_ref, basis_ref,
    term_ref, own_update_ref, other_update_ref, screened_ref, near_ref,
    screen_ref, far_ref, field_ref, far_sems, near_sem,
):
    steps, _, width = far_ref.shape
    far, near = 1 - upper_half(), upper_half()

    def fetch(half, step, held_ref, sem):
        start = pl.multiple_of((half * steps + step) * width, width)
        return pltpu.make_async_copy(
            basis_ref.at[:, pl.ds(start, width)], held_ref.at[step], sem
        )

    for step in range(steps):
        fetch(far, step, far_ref, far_sems.at[step]).start()
    screen_coeffs(coeffs_ref, packed_ref, screen_ref, screened_ref)
    for step in range(steps):
        fetch(near, step, near_ref, near_sem.at[step]).start()
    respond_half(
        screened_ref, far_ref, field_ref, (occ_ref, own_ref, other_ref),
        (term_ref, own_update_ref, other_update_ref), far,
        lambda step: fetch(far, step, far_ref, far_sems.at[step]).wait(),
    )
    for step in range(steps):
        fetch(near, step, near_ref, near_sem.at[step]).wait()


def respond_near_kernel(
    screened_ref, occ_ref, own_ref, other_ref, near_ref,
    term_ref, own_update_ref, other_update_ref, field_ref,
):
    respond_half(
        screened_ref, near_ref, field_ref, (occ_ref, own_ref, other_ref),
        (term_ref, own_update_ref, other_update_ref), upper_half(),
    )


def respond(coeffs, packed, basis, near_occ, far_occ, own, other):
    local_k, occ_count, half = near_occ.shape
    grid_count = 2 * half
    group_count = own.shape[1]
    rows, aux_count = coeffs.shape
    width = min(1024, half)
    any_spec = pl.BlockSpec(memory_space=pl.ANY)
    shapes = [
        jax.ShapeDtypeStruct((local_k, occ_count, half), BF16),
        jax.ShapeDtypeStruct((local_k, group_count, half), BF16),
        jax.ShapeDtypeStruct((local_k, group_count, half), BF16),
    ]
    held = (half // width, aux_count, width)
    cost = pl.CostEstimate(
        flops=rows * grid_count * aux_count, bytes_accessed=4 << 20, transcendentals=0
    )
    *far, screened, near_basis = pl.pallas_call(
        respond_far_kernel,
        in_specs=[VMEM_SPEC] * 5 + [any_spec],
        out_specs=[VMEM_SPEC] * 5,
        out_shape=shapes
        + [jax.ShapeDtypeStruct(coeffs.shape, BF16), jax.ShapeDtypeStruct(held, BF16)],
        scratch_shapes=[
            pltpu.VMEM((aux_count, aux_count), BF16),
            pltpu.VMEM(held, BF16),
            pltpu.VMEM((rows, width), BF16),
            pltpu.SemaphoreType.DMA((held[0],)),
            pltpu.SemaphoreType.DMA((held[0],)),
        ],
        compiler_params=pltpu.CompilerParams(vmem_limit_bytes=FAR_VMEM),
        cost_estimate=cost,
        name="respond_far",
    )(coeffs, packed, far_occ, own, other, basis)
    near = pl.pallas_call(
        respond_near_kernel,
        in_specs=[VMEM_SPEC] * 5,
        out_specs=[VMEM_SPEC] * 3,
        out_shape=shapes,
        scratch_shapes=[pltpu.VMEM((rows, width), BF16)],
        compiler_params=pltpu.CompilerParams(vmem_limit_bytes=NEAR_VMEM),
        cost_estimate=cost,
        name="respond_near",
    )(screened, near_occ, own, other, near_basis)
    return far, near


def shards(occupied, virtual, occ_energy, virt_energy, partner, coulomb, basis):
    local_k, occ_count, grid_count = occupied.shape
    group_count = virtual.shape[1]
    aux_count = basis.shape[0]
    transfers = partner.shape[0]
    assert transfers == 2
    cube = Hypercube()
    total_k = local_k * cube.ka
    virt_count = group_count * cube.band
    gram_scale = 1.0 / math.sqrt(total_k * occ_count * virt_count * aux_count)
    occ_scale = 1.0 / math.sqrt(transfers * virt_count)
    ka = lax.axis_index("ka")

    other_virtual = cube.swap(virtual, cube.core)
    other_energy = cube.swap(virt_energy, cube.core)

    def operands(late_ka, late_band):
        def level_rows(energy):
            rows = lax.dynamic_slice_in_dim(energy, late_ka * local_k, local_k, axis=0)
            return jnp.broadcast_to(rows[:, :, None], rows.shape + (LANES,))

        levels = jnp.concatenate([level_rows(virt_energy), level_rows(other_energy)])
        near_start = (late_band // 2) % 2 * (grid_count // 2)
        first_basis = lax.dynamic_slice_in_dim(basis, near_start, grid_count // 8, axis=1)
        return levels, first_basis

    sources = partners_of(partner, ka, local_k)
    neighbour_sources = partners_of(partner, jnp.bitwise_xor(ka, 1), local_k)
    near_occ, far_occ, partner_energy, (levels, first_basis) = fetch_partners(
        cube, occupied, occ_energy, sources, neighbour_sources, operands
    )
    partner_energy = jnp.broadcast_to(
        partner_energy[:, :, None], partner_energy.shape + (LANES,)
    )
    coeffs, packed = project(
        near_occ, far_occ, virtual, other_virtual, first_basis, basis, partner_energy, levels, coulomb,
        gram_scale,
    )
    packed = reduce_screen(cube, packed)
    far, near = respond(coeffs, packed, basis, near_occ, far_occ, virtual, other_virtual)
    arrived = cube.swap(far[0], cube.y)
    terms = (near[0].astype(F32) + arrived.astype(F32)).astype(BF16)
    updates = [
        (own.astype(F32) + cube.swap(other, cube.core).astype(F32)).astype(BF16)
        for _, own, other in (far, near)
    ]
    lower = cube.bit(cube.y) == 0
    virt_update = jnp.concatenate(
        [jnp.where(lower, updates[1], updates[0]), jnp.where(lower, updates[0], updates[1])],
        axis=2,
    )
    occ_total, virt_update = return_occupied(
        cube, terms, local_k, sources, neighbour_sources, virt_update
    )
    return ((occ_total * occ_scale).astype(BF16), virt_update)


def solution(mesh):
    in_specs = (
        P("ka", None, None),
        P("ka", "band", None),
        P("ka", None),
        P(None, "band"),
        P(),
        P(),
        P(),
    )
    out_specs = (P("ka", None, "band"), P("ka", "band", None))
    return jax.shard_map(shards, mesh=mesh, in_specs=in_specs, out_specs=out_specs, check_vma=False)
```

```python
import functools
import math

import jax
import jax.numpy as jnp
from jax import lax
from jax.experimental import pallas as pl
from jax.experimental.pallas import tpu as pltpu
from jax.sharding import PartitionSpec as P


FREQUENCY = 2.5
BROADENING = 0.4
LANES = 128
PROJECT_VMEM = 48 << 20
FAR_VMEM = 45 << 20
NEAR_VMEM = 32 << 20
VMEM_SPEC = pl.BlockSpec(memory_space=pltpu.VMEM)
BF16 = jnp.bfloat16
F32 = jnp.float32


def response(energy_gaps):
    shifted = FREQUENCY - energy_gaps
    return shifted / (shifted * shifted + BROADENING * BROADENING)


def pick(stack, index):
    return lax.dynamic_index_in_dim(stack, index, 0, keepdims=False)


class Hypercube:
    def __init__(self):
        self.ka = lax.axis_size("ka")
        self.band = lax.axis_size("band")
        self.count = self.ka * self.band
        assert self.band == 4 and self.ka >= 2 and self.ka & (self.ka - 1) == 0
        self.index = lax.axis_index("ka") * self.band + lax.axis_index("band")
        self.core, self.y, self.x = 1, 2, 4
        rest = [bit for bit in (1 << n for n in range(3, 31)) if bit < self.count]
        self.groups = [rest[n : n + 2] for n in range(0, len(rest), 2)]

    def bit(self, mask):
        return (self.index // mask) % 2

    def swap(self, value, mask):
        return lax.ppermute(
            value, ("ka", "band"), [(device, device ^ mask) for device in range(self.count)]
        )


def masks_of(bits):
    return [sum(bit for n, bit in enumerate(bits) if (d >> n) & 1) for d in range(1, 1 << len(bits))]


def sum_scatter(cube, parts, bits):
    me = sum(cube.bit(bit) << n for n, bit in enumerate(bits))
    total = pick(parts, me).astype(F32)
    arrived = []
    for d, mask in enumerate(masks_of(bits)):
        arrived.append(cube.swap(pick(parts, jnp.bitwise_xor(me, d + 1)), mask))
    for term in arrived:
        total = total + term.astype(F32)
    return total


def gather_differences(cube, value, bits):
    return jnp.stack([value] + [cube.swap(value, mask) for mask in masks_of(bits)])


def gather_parts(cube, value, bits):
    me = sum(cube.bit(bit) << n for n, bit in enumerate(bits))
    differences = gather_differences(cube, value, bits)
    return jnp.stack(
        [pick(differences, jnp.bitwise_xor(me, d)) for d in range(1 << len(bits))]
    )


def blocks_of(aux_count):
    count = aux_count // LANES
    return [(row, column) for row in range(count) for column in range(row + 1, count)]


def packed_rows(aux_count):
    count = aux_count // LANES
    assert count % 2 == 0
    blocks = (len(blocks_of(aux_count)) + count // 2) * LANES
    return blocks, blocks + 64


def split_float(value):
    high = lax.reduce_precision(value, 8, 7)
    middle = lax.reduce_precision(value - high, 8, 7)
    low = value - high - middle
    return high.astype(BF16), middle.astype(BF16), low.astype(BF16)


def partners_of(partner, device, local_k):
    every_k = jnp.arange(partner.shape[1], dtype=jnp.int32)
    own_k = device * local_k + jnp.arange(local_k, dtype=jnp.int32)
    here = every_k[None, None, :] == own_k[None, :, None]
    return jnp.sum(jnp.where(here, partner[:, None, :], 0), axis=2).reshape(-1)


def own_transfer_first(cube, values, local_k):
    first = cube.bit(cube.core) == 0
    low, high = values[:local_k], values[local_k:]
    return jnp.where(first, low, high), jnp.where(first, high, low)


def fetch_partners(cube, occupied, occ_energy, sources, neighbour_sources, make_beside):
    local_k, _, grid_count = occupied.shape
    width = grid_count // cube.band
    ka = lax.axis_index("ka")
    first = cube.bit(cube.core) == 0
    quarter = lax.dynamic_slice_in_dim(occupied, lax.axis_index("band") * width, width, axis=2)
    pieces = jnp.stack(split_float(occ_energy), axis=2)
    payload = jnp.concatenate(
        [quarter, jnp.pad(pieces, ((0, 0), (0, 0), (0, LANES - pieces.shape[2])))], axis=2
    )
    gathered = payload[None]
    for bits in cube.groups:
        gathered = gather_differences(cube, gathered, bits).reshape((-1,) + payload.shape)
    gathered = gathered.reshape((-1,) + payload.shape[1:])
    gathered, late_ka, late_band = lax.optimization_barrier((gathered, ka, lax.axis_index("band")))
    beside = make_beside(late_ka, late_band)
    side, upper = ka % 2, ka // 2
    slots = jnp.arange(gathered.shape[0], dtype=jnp.int32)
    held = (jnp.bitwise_xor(slots // local_k, upper) * 2 + side) * local_k + slots % local_k

    def held_of(wanted):
        hits = wanted[:, None] == held[None, :]
        return jnp.sum(
            jnp.where(hits[:, :, None, None], gathered[None].astype(F32), 0.0), axis=1
        ).astype(BF16)

    own_sources, other_sources = own_transfer_first(cube, sources, local_k)
    own_neighbour, other_neighbour = own_transfer_first(cube, neighbour_sources, local_k)
    along_x = cube.swap(held_of(own_neighbour), cube.x)
    across = cube.swap(held_of(other_neighbour)[:, :, :width], cube.x | cube.core)
    beside_core = cube.swap(held_of(other_sources)[:, :, :width], cube.core)
    along_x, beside = lax.optimization_barrier((along_x, beside))
    mine = held_of(own_sources) + along_x
    other = beside_core + across
    energy = mine[:, :, width : width + 3].astype(F32)
    energy = (energy[:, :, 0] + energy[:, :, 1]) + energy[:, :, 2]
    part = mine[:, :, :width]
    part = jnp.concatenate([jnp.where(first, part, other), jnp.where(first, other, part)], axis=2)
    return part, cube.swap(part, cube.y), energy, beside


def reduce_screen(cube, own):
    rows = own.shape[0]
    piece = sum_scatter(cube, own.reshape(4, rows // 4, LANES), [cube.y, cube.x]).astype(BF16)
    for bits in cube.groups:
        arrived = [cube.swap(piece, mask) for mask in masks_of(bits)]
        total = piece.astype(F32)
        for term in arrived:
            total = total + term.astype(F32)
        piece = total.astype(BF16)
    return gather_parts(cube, piece, [cube.y, cube.x]).reshape(own.shape)


def return_occupied(cube, part, local_k, sources, neighbour_sources, beside):
    ka = lax.axis_index("ka")
    width = part.shape[2] // 2
    first = cube.bit(cube.core) == 0
    keep = jnp.where(first, part[:, :, :width], part[:, :, width:])
    give = jnp.where(first, part[:, :, width:], part[:, :, :width])
    along_x = cube.swap(keep, cube.x)
    across = cube.swap(give, cube.x | cube.core)
    beside_core = cube.swap(give, cube.core)
    side, upper = ka % 2, ka // 2
    both = jnp.concatenate([keep, beside_core, along_x, across], axis=0)
    targets = jnp.concatenate(
        own_transfer_first(cube, sources, local_k)
        + own_transfer_first(cube, neighbour_sources, local_k)
    )

    def placed(uppers):
        wanted_k = ((uppers * 2 + side) * local_k)[:, None] + jnp.arange(local_k, dtype=jnp.int32)
        hits = targets[None, None, :] == wanted_k[:, :, None]
        return jnp.sum(
            jnp.where(hits[:, :, :, None, None], both[None, None].astype(F32), 0.0), axis=2
        )

    spans = 1
    for bits in cube.groups:
        spans *= 1 << len(bits)
    differences = jnp.arange(spans, dtype=jnp.int32)
    value = placed(jnp.bitwise_xor(differences, upper))
    for bits in reversed(cube.groups):
        size = 1 << len(bits)
        value = value.reshape((size, -1) + value.shape[1:])
        total = value[0]
        arrived = [
            cube.swap(value[d + 1].astype(BF16), mask) for d, mask in enumerate(masks_of(bits))
        ]
        arrived[-1], beside = lax.optimization_barrier((arrived[-1], beside))
        for term in arrived:
            total = total + term.astype(F32)
        value = total
    return value[0], beside


def pair_coeffs(occ, virt, basis):
    pair_rows = jnp.concatenate([occ[i : i + 1] * virt for i in range(occ.shape[0])], axis=0)
    return lax.dot_general(
        pair_rows, basis, (((1,), (1,)), ((), ())), preferred_element_type=F32
    )


def upper_half():
    return (lax.axis_index("band") // 2) % 2


def project_near_kernel(
    occ_ref, own_ref, other_ref, first_ref, basis_ref, total_ref, far_ref, held_ref, sems, *, starts
):
    local_k, occ_count, half = occ_ref.shape
    rows = occ_count * own_ref.shape[1]
    near = pl.multiple_of(upper_half() * half, half)
    far = pl.multiple_of((1 - upper_half()) * half, half)
    parts = list(zip(starts, starts[1:] + (half,)))
    offset = starts[1]
    copies = [
        pltpu.make_async_copy(
            basis_ref.at[:, pl.ds(near + start, end - start)],
            held_ref.at[:, start - offset : end - offset],
            sems.at[n],
        )
        for n, (start, end) in enumerate(parts[1:])
    ]
    copies.append(
        pltpu.make_async_copy(basis_ref.at[:, pl.ds(far, half)], far_ref, sems.at[len(copies)])
    )
    for copy in copies:
        copy.start()
    terms = [(virt_ref, k) for virt_ref in (own_ref, other_ref) for k in range(local_k)]
    for n, (start, end) in enumerate(parts):
        if n > 0:
            copies[n - 1].wait()
        for term, (virt_ref, k) in enumerate(terms):
            part = pair_coeffs(
                occ_ref[k, :, start:end],
                virt_ref[k, :, pl.ds(near + start, end - start)],
                held_ref[:, start - offset : end - offset] if n > 0 else first_ref[...],
            )
            here = slice(term * rows, (term + 1) * rows)
            total_ref[here, :] = total_ref[here, :] + part if n > 0 else part
    copies[-1].wait()


def project_kernel(
    occ_ref, own_ref, other_ref, occ_energy_ref, levels_ref, coulomb_ref, total_ref, basis_ref,
    coeffs_ref, gram_ref, weighted_ref, *, scale,
):
    local_k, occ_count, half = occ_ref.shape
    group_count = own_ref.shape[1]
    aux_count = basis_ref.shape[0]
    rows = occ_count * group_count
    count = aux_count // LANES
    far = pl.multiple_of((1 - upper_half()) * half, half)
    terms = [(virt_ref, k) for virt_ref in (own_ref, other_ref) for k in range(local_k)]
    for term, (virt_ref, k) in enumerate(terms):
        here = slice(term * rows, (term + 1) * rows)
        part = pair_coeffs(occ_ref[k], virt_ref[k, :, pl.ds(far, half)], basis_ref[...])
        coeffs = (total_ref[here, :] + part).astype(BF16)
        coeffs_ref[here, :] = coeffs
        for i in range(occ_count):
            first = i * group_count
            weights = response(levels_ref[term] - occ_energy_ref[k][i : i + 1])
            values = coeffs[first : first + group_count].astype(F32)
            weighted_ref[term * rows + first : term * rows + first + group_count, :] = (
                jnp.concatenate(
                    [values[:, n * LANES : (n + 1) * LANES] * weights for n in range(count)],
                    axis=1,
                ).astype(BF16)
            )
    coulomb = coulomb_ref[...] * math.sqrt(scale)
    tiles = {}
    for panel in range(0, count, 2):
        gram = lax.dot_general(
            weighted_ref[:, panel * LANES : (panel + 2) * LANES],
            coeffs_ref[:, panel * LANES :],
            (((0,), (0,)), ((), ())),
            preferred_element_type=F32,
        )
        for row in (panel, panel + 1):
            left = jnp.broadcast_to(coulomb[:, row * LANES : (row + 1) * LANES], (LANES, LANES)).T
            for column in range(row, count):
                down, across = (row - panel) * LANES, (column - panel) * LANES
                right = coulomb[:, column * LANES : (column + 1) * LANES]
                tiles[row, column] = (
                    left * gram[down : down + LANES, across : across + LANES] * right
                )
    places = blocks_of(aux_count)
    for n, place in enumerate(places):
        gram_ref[n * LANES : (n + 1) * LANES, :] = tiles[place].astype(BF16)
    down = lax.broadcasted_iota(jnp.int32, (LANES, LANES), 0)
    across = lax.broadcasted_iota(jnp.int32, (LANES, LANES), 1)
    lines = []
    for pair in range(count // 2):
        upper, lower = tiles[2 * pair, 2 * pair], tiles[2 * pair + 1, 2 * pair + 1]
        n = len(places) + pair
        gram_ref[n * LANES : (n + 1) * LANES, :] = jnp.where(across >= down, upper, lower).astype(
            BF16
        )
        lines.append(jnp.sum(jnp.where(across == down, lower, 0.0), axis=0, keepdims=True))
    blocks, total_rows = packed_rows(aux_count)
    lines.append(jnp.zeros((total_rows - blocks - len(lines), LANES), F32))
    gram_ref[blocks:, :] = jnp.concatenate(lines, axis=0).astype(BF16)


def project(near_occ, far_occ, own, other, first, basis, occ_energy, levels, coulomb, scale):
    local_k, occ_count, half = near_occ.shape
    group_count = own.shape[1]
    aux_count = basis.shape[0]
    rows = 2 * local_k * occ_count * group_count
    width = first.shape[1]
    starts = (0, width, 2 * width)
    cost = pl.CostEstimate(
        flops=2 * rows * half * aux_count, bytes_accessed=4 << 20, transcendentals=0
    )
    total, far_basis = pl.pallas_call(
        functools.partial(project_near_kernel, starts=starts),
        in_specs=[VMEM_SPEC] * 4 + [pl.BlockSpec(memory_space=pl.ANY)],
        out_specs=[VMEM_SPEC] * 2,
        out_shape=[
            jax.ShapeDtypeStruct((rows, aux_count), F32),
            jax.ShapeDtypeStruct((aux_count, half), BF16),
        ],
        scratch_shapes=[
            pltpu.VMEM((aux_count, half - width), BF16),
            pltpu.SemaphoreType.DMA((len(starts),)),
        ],
        compiler_params=pltpu.CompilerParams(vmem_limit_bytes=PROJECT_VMEM),
        cost_estimate=cost,
        name="project_near",
    )(near_occ, own, other, first, basis)
    return pl.pallas_call(
        functools.partial(project_kernel, scale=scale),
        in_specs=[VMEM_SPEC] * 8,
        out_specs=[VMEM_SPEC] * 2,
        out_shape=[
            jax.ShapeDtypeStruct((rows, aux_count), BF16),
            jax.ShapeDtypeStruct((packed_rows(aux_count)[1], LANES), BF16),
        ],
        scratch_shapes=[pltpu.VMEM((rows, aux_count), BF16)],
        compiler_params=pltpu.CompilerParams(vmem_limit_bytes=NEAR_VMEM),
        cost_estimate=cost,
        name="project",
    )(far_occ, own, other, occ_energy, levels, coulomb, total, far_basis)


def screen_coeffs(coeffs_ref, packed_ref, screen_ref, screened_ref):
    aux_count = coeffs_ref.shape[1]
    places = blocks_of(aux_count)
    for n, (row, column) in enumerate(places):
        tile = packed_ref[n * LANES : (n + 1) * LANES, :]
        upper = slice(row * LANES, (row + 1) * LANES)
        lower = slice(column * LANES, (column + 1) * LANES)
        screen_ref[upper, lower] = tile
        screen_ref[lower, upper] = tile.T
    down = lax.broadcasted_iota(jnp.int32, (LANES, LANES), 0)
    across = lax.broadcasted_iota(jnp.int32, (LANES, LANES), 1)
    lines = packed_ref[packed_rows(aux_count)[0] :, :].astype(F32)
    for pair in range(aux_count // LANES // 2):
        n = len(places) + pair
        tile = packed_ref[n * LANES : (n + 1) * LANES, :].astype(F32)
        turned = tile.T
        first = slice(2 * pair * LANES, (2 * pair + 1) * LANES)
        second = slice((2 * pair + 1) * LANES, (2 * pair + 2) * LANES)
        screen_ref[first, first] = jnp.where(across >= down, tile, turned).astype(BF16)
        strict = jnp.where(across < down, tile, turned)
        screen_ref[second, second] = jnp.where(
            across == down, lines[pair : pair + 1], strict
        ).astype(BF16)
    screened_ref[...] = jnp.dot(
        coeffs_ref[...], screen_ref[...], preferred_element_type=F32
    ).astype(BF16)


def respond_half(screened_ref, held_ref, field_ref, inputs, outs, half, arrived=None):
    occ_ref, own_ref, other_ref = inputs
    term_ref, own_update_ref, other_update_ref = outs
    local_k, occ_count, _ = occ_ref.shape
    group_count = own_ref.shape[1]
    rows = occ_count * group_count
    span = term_ref.shape[2]
    width = held_ref.shape[2]

    def grid_of(step):
        return pl.ds(pl.multiple_of(half * span + step * width, width), width)

    def chunk(step, carry):
        to = pl.ds(pl.multiple_of(step * width, width), width)
        grid = grid_of(step)
        if arrived is not None:
            arrived(step)
        field_ref[...] = jnp.dot(
            screened_ref[...], held_ref[step], preferred_element_type=F32
        ).astype(BF16)
        for k in range(local_k):
            occ = occ_ref[k, :, to].astype(F32)
            sums = [None] * occ_count
            sides = ((own_ref, own_update_ref), (other_ref, other_update_ref))
            for side, (virt_ref, update_ref) in enumerate(sides):
                virt = virt_ref[k, :, grid].astype(F32)
                first = (side * local_k + k) * rows
                virt_term = None
                for i in range(occ_count):
                    here = slice(first + i * group_count, first + (i + 1) * group_count)
                    piece = field_ref[here, :].astype(F32)
                    line = jnp.sum((piece * virt).reshape(group_count // 8, 8, width), axis=0)
                    sums[i] = line if side == 0 else sums[i] + line
                    product = piece * occ[i : i + 1]
                    virt_term = product if virt_term is None else virt_term + product
                update_ref[k, :, to] = virt_term.astype(BF16)
            term_ref[k, :, to] = jnp.concatenate(
                [jnp.sum(line, axis=0, keepdims=True) for line in sums], axis=0
            ).astype(BF16)
        return carry

    lax.fori_loop(0, span // width, chunk, 0)


def respond_far_kernel(
    coeffs_ref, packed_ref, occ_ref, own_ref, other_ref, basis_ref,
    term_ref, own_update_ref, other_update_ref, screened_ref, near_ref,
    screen_ref, far_ref, field_ref, far_sems, near_sem,
):
    steps, _, width = far_ref.shape
    far, near = 1 - upper_half(), upper_half()

    def fetch(half, step, held_ref, sem):
        start = pl.multiple_of((half * steps + step) * width, width)
        return pltpu.make_async_copy(
            basis_ref.at[:, pl.ds(start, width)], held_ref.at[step], sem
        )

    for step in range(steps):
        fetch(far, step, far_ref, far_sems.at[step]).start()
    for step in range(steps):
        fetch(near, step, near_ref, near_sem.at[step]).start()
    screen_coeffs(coeffs_ref, packed_ref, screen_ref, screened_ref)
    respond_half(
        screened_ref, far_ref, field_ref, (occ_ref, own_ref, other_ref),
        (term_ref, own_update_ref, other_update_ref), far,
        lambda step: fetch(far, step, far_ref, far_sems.at[step]).wait(),
    )
    for step in range(steps):
        fetch(near, step, near_ref, near_sem.at[step]).wait()


def respond_near_kernel(
    screened_ref, occ_ref, own_ref, other_ref, near_ref,
    term_ref, own_update_ref, other_update_ref, field_ref,
):
    respond_half(
        screened_ref, near_ref, field_ref, (occ_ref, own_ref, other_ref),
        (term_ref, own_update_ref, other_update_ref), upper_half(),
    )


def respond(coeffs, packed, basis, near_occ, far_occ, own, other):
    local_k, occ_count, half = near_occ.shape
    grid_count = 2 * half
    group_count = own.shape[1]
    rows, aux_count = coeffs.shape
    width = min(1024, half)
    any_spec = pl.BlockSpec(memory_space=pl.ANY)
    shapes = [
        jax.ShapeDtypeStruct((local_k, occ_count, half), BF16),
        jax.ShapeDtypeStruct((local_k, group_count, half), BF16),
        jax.ShapeDtypeStruct((local_k, group_count, half), BF16),
    ]
    held = (half // width, aux_count, width)
    cost = pl.CostEstimate(
        flops=rows * grid_count * aux_count, bytes_accessed=4 << 20, transcendentals=0
    )
    *far, screened, near_basis = pl.pallas_call(
        respond_far_kernel,
        in_specs=[VMEM_SPEC] * 5 + [any_spec],
        out_specs=[VMEM_SPEC] * 5,
        out_shape=shapes
        + [jax.ShapeDtypeStruct(coeffs.shape, BF16), jax.ShapeDtypeStruct(held, BF16)],
        scratch_shapes=[
            pltpu.VMEM((aux_count, aux_count), BF16),
            pltpu.VMEM(held, BF16),
            pltpu.VMEM((rows, width), BF16),
            pltpu.SemaphoreType.DMA((held[0],)),
            pltpu.SemaphoreType.DMA((held[0],)),
        ],
        compiler_params=pltpu.CompilerParams(vmem_limit_bytes=FAR_VMEM),
        cost_estimate=cost,
        name="respond_far",
    )(coeffs, packed, far_occ, own, other, basis)
    near = pl.pallas_call(
        respond_near_kernel,
        in_specs=[VMEM_SPEC] * 5,
        out_specs=[VMEM_SPEC] * 3,
        out_shape=shapes,
        scratch_shapes=[pltpu.VMEM((rows, width), BF16)],
        compiler_params=pltpu.CompilerParams(vmem_limit_bytes=NEAR_VMEM),
        cost_estimate=cost,
        name="respond_near",
    )(screened, near_occ, own, other, near_basis)
    return far, near


def shards(occupied, virtual, occ_energy, virt_energy, partner, coulomb, basis):
    local_k, occ_count, grid_count = occupied.shape
    group_count = virtual.shape[1]
    aux_count = basis.shape[0]
    transfers = partner.shape[0]
    assert transfers == 2
    cube = Hypercube()
    total_k = local_k * cube.ka
    virt_count = group_count * cube.band
    gram_scale = 1.0 / math.sqrt(total_k * occ_count * virt_count * aux_count)
    occ_scale = 1.0 / math.sqrt(transfers * virt_count)
    ka = lax.axis_index("ka")

    other_virtual = cube.swap(virtual, cube.core)
    other_energy = cube.swap(virt_energy, cube.core)

    def operands(late_ka, late_band):
        def level_rows(energy):
            rows = lax.dynamic_slice_in_dim(energy, late_ka * local_k, local_k, axis=0)
            return jnp.broadcast_to(rows[:, :, None], rows.shape + (LANES,))

        levels = jnp.concatenate([level_rows(virt_energy), level_rows(other_energy)])
        near_start = (late_band // 2) % 2 * (grid_count // 2)
        first_basis = lax.dynamic_slice_in_dim(basis, near_start, grid_count // 8, axis=1)
        factors = jnp.where(late_band % 2 == 0, coulomb[:1], coulomb[1:])
        return levels, first_basis, factors

    sources = partners_of(partner, ka, local_k)
    neighbour_sources = partners_of(partner, jnp.bitwise_xor(ka, 1), local_k)
    near_occ, far_occ, partner_energy, (levels, first_basis, factors) = fetch_partners(
        cube, occupied, occ_energy, sources, neighbour_sources, operands
    )
    partner_energy = jnp.broadcast_to(
        partner_energy[:, :, None], partner_energy.shape + (LANES,)
    )
    coeffs, packed = project(
        near_occ, far_occ, virtual, other_virtual, first_basis, basis, partner_energy, levels, factors,
        gram_scale,
    )
    packed = reduce_screen(cube, packed)
    far, near = respond(coeffs, packed, basis, near_occ, far_occ, virtual, other_virtual)
    arrived = cube.swap(far[0], cube.y)
    terms = (near[0].astype(F32) + arrived.astype(F32)).astype(BF16)
    updates = [
        (own.astype(F32) + cube.swap(other, cube.core).astype(F32)).astype(BF16)
        for _, own, other in (far, near)
    ]
    lower = cube.bit(cube.y) == 0
    virt_update = jnp.concatenate(
        [jnp.where(lower, updates[1], updates[0]), jnp.where(lower, updates[0], updates[1])],
        axis=2,
    )
    occ_total, virt_update = return_occupied(
        cube, terms, local_k, sources, neighbour_sources, virt_update
    )
    return ((occ_total * occ_scale).astype(BF16), virt_update)


def solution(mesh):
    in_specs = (
        P("ka", None, None),
        P("ka", "band", None),
        P("ka", None),
        P(None, "band"),
        P(),
        P(),
        P(),
    )
    out_specs = (P("ka", None, "band"), P("ka", "band", None))

    return jax.shard_map(shards, mesh=mesh, in_specs=in_specs, out_specs=out_specs, check_vma=False)
```
